256 devices in a mesh: tm: 8 (over x, core), stn: 32 (over z, y).
Axes of the slice: x: 4, y: 4, z: 8, core: 2. Of those that a mesh axis runs over, the one named last changes fastest.
Arguments:
- voltages: bfloat16 [512, 2, 165888], P('stn', None, 'tm'), may hold values from -6 to 6
- prototype: float32 [12, 768], replicated, may hold values from -1.75 to 1.75
- kept_channels: int32 [64], replicated, may hold values from 0 to 383, as said below
- beam_jones: float32 [512, 2, 2, 2, 64], P('stn'), may hold values from -3 to 3
- station_map: int32 [512], replicated, may hold values from 0 to 511, each once
- tile_pairs: int32 [36, 2], replicated, may hold values from 0 to 7, as said below
Outputs:
- visibilities: float32 [256, 36, 2, 128, 128], P(('tm', 'stn'))
The draws below stay inside these ranges and needn't reach their ends.
Inputs may be any that keep to these rules, and one draw needn't show every extreme that they name: `kept_channels`: distinct coarse channel numbers in no particular order; channel 0 and the highest channel are always among them. Each row of voltages and beam_jones belongs to station station_map[row]; every station once. `tile_pairs`: every unordered pair of signal blocks, a block with itself included, stands in exactly one row, in either order.
All inputs are finite; a program needn't handle non-finite values.
Results may differ from the reference program's by a relative error of at most 0.0037.
Values may be sent and summed in bfloat16 or wider, within the bound.
No kernel may reach another device: no remote copies, remote signals or barrier semaphores. Data moves between devices by JAX's collectives and lax.ppermute only.
A program may use at most 64 MiB of HBM per device.

```python
import math
import jax
import jax.numpy as jnp
import numpy as np
from jax import lax

STATIONS = 512
FRAME = 768
TAPS = 12
KEPT = 64
FINE = 216
GROUP = 54
BLOCK = 128
SAMPLES = 165888
SIGNALS = 1024
NBLK = 8
TILES = 36
OUT_CH = 256


def draw_kept_channels(key, part):
    middle = jax.random.permutation(key, FRAME // 2 - 2) + 1
    ends = jnp.array([0, FRAME // 2 - 1], jnp.int32)
    chosen = jnp.concatenate([ends, middle[:KEPT - 2].astype(jnp.int32)])
    shuffle = jax.random.permutation(jax.random.fold_in(key, 7), KEPT)
    return chosen[shuffle].astype(jnp.int32)


def draw_tile_pairs(key, part):
    upper_rows, upper_cols = np.triu_indices(NBLK)
    first_block = jnp.asarray(upper_rows, jnp.int32)
    second_block = jnp.asarray(upper_cols, jnp.int32)
    shuffle = jax.random.permutation(key, TILES)
    flipped = jax.random.randint(jax.random.fold_in(key, 11), (TILES,), 0, 2)
    left_block = jnp.where(flipped == 1, second_block, first_block)[shuffle]
    right_block = jnp.where(flipped == 1, first_block, second_block)[shuffle]
    return jnp.stack([left_block, right_block], axis=1).astype(jnp.int32)


def shard_levels(key, shape, pieces, low, top_value):
    gain, own = 1.0, jax.random.fold_in(key, 6)
    for axis_at, blocks in pieces:
        steps = jnp.exp(jax.random.uniform(jax.random.fold_in(own, axis_at), (blocks,), jnp.float32, low / len(pieces), top_value / len(pieces)))
        gain = gain * jnp.repeat(steps, shape[axis_at] // blocks).reshape([-1 if axis == axis_at else 1 for axis in range(len(shape))])
    return gain


def gaussian(stream_key, extent, scale, limit, split=(), kind=jnp.bfloat16):
    gain = shard_levels(stream_key, extent, split, -0.22, 0.18) if split else 1.0
    result = jax.random.normal(stream_key, extent, jnp.float32) * scale * gain
    return jnp.minimum(jnp.maximum(result, -limit), limit).astype(kind)


def setup_inputs(seed: int = 0) -> dict:
    splits = jax.random.split(jax.random.key(seed), 7)
    return {
        "voltages": gaussian(splits[0], (STATIONS, 2, SAMPLES), 1.0, 6.0, ((0, 32), (2, 8))),
        "prototype": gaussian(splits[1], (TAPS, FRAME), TAPS ** -0.5, 1.75, (), jnp.float32),
        "kept_channels": draw_kept_channels(jax.random.fold_in(splits[6], 71), 0),
        "beam_jones": gaussian(splits[3], (STATIONS, 2, 2, 2, KEPT), 0.5, 3.0, ((0, 32),), jnp.float32),
        "station_map": jax.random.permutation(splits[4], STATIONS).astype(jnp.int32),
        "tile_pairs": draw_tile_pairs(jax.random.fold_in(splits[6], 71), 0),
    }


PRECISE = lax.Precision.HIGHEST

def reference(voltages, prototype, kept_channels, beam_jones, station_map, tile_pairs):

    def per_station(packed):
        samples, weights = packed
        series = samples.reshape(2, FINE, FRAME).astype(jnp.float32)
        padded = jnp.concatenate([jnp.zeros((2, TAPS - 1, FRAME), jnp.float32), series], axis=1)
        filtered = jnp.zeros((2, FINE, FRAME), jnp.float32)
        for offset in range(TAPS):
            filtered = filtered + prototype[offset][None, None, :] * padded[:, offset:offset + FINE, :]
        spectrum = jnp.take(jnp.fft.rfft(filtered, axis=-1), kept_channels, axis=-1) / math.sqrt(FRAME)
        coarse_re = jnp.real(spectrum)[None]
        coarse_im = jnp.imag(spectrum)[None]
        jones_re = weights[:, :, 0, :][:, :, None, :]
        jones_im = weights[:, :, 1, :][:, :, None, :]
        beam_re = lax.optimization_barrier(jnp.sum(jones_re * coarse_re - jones_im * coarse_im, axis=1))
        beam_im = lax.optimization_barrier(jnp.sum(jones_re * coarse_im + jones_im * coarse_re, axis=1))
        beam_re = lax.optimization_barrier(beam_re.astype(jnp.bfloat16)).astype(jnp.float32)
        beam_im = lax.optimization_barrier(beam_im.astype(jnp.bfloat16)).astype(jnp.float32)
        fine = jnp.fft.fft(lax.complex(beam_re, beam_im), axis=1) / math.sqrt(FINE)
        return jnp.stack([jnp.real(fine), jnp.imag(fine)], axis=1)
    fine_all = lax.map(per_station, (voltages, beam_jones))
    row_of = jnp.zeros((STATIONS,), jnp.int32).at[station_map].set(jnp.arange(STATIONS, dtype=jnp.int32))
    ordered = fine_all[row_of]
    grouped = ordered.reshape(STATIONS, 2, 2, FINE // GROUP, GROUP, KEPT)
    grouped = jnp.transpose(grouped, (5, 3, 0, 1, 2, 4)).reshape(OUT_CH, SIGNALS, 2 * GROUP)

    def correlate(channel_rows):
        blocks = channel_rows.reshape(NBLK, BLOCK, 2 * GROUP)
        left_rows = blocks[tile_pairs[:, 0]]
        right_rows = blocks[tile_pairs[:, 1]]
        swapped = jnp.concatenate([left_rows[..., GROUP:], -left_rows[..., :GROUP]], axis=-1)
        real_part = jnp.einsum('tax,tbx->tab', left_rows, right_rows, precision=PRECISE)
        imag_part = jnp.einsum('tax,tbx->tab', swapped, right_rows, precision=PRECISE)
        return jnp.stack([real_part, imag_part], axis=1) / GROUP
    return lax.map(correlate, grouped)
```

```python
import functools
import math

import jax
import jax.numpy as jnp
import numpy as np
from jax import lax
from jax.experimental import pallas as pl
from jax.experimental.pallas import tpu as pltpu
from jax.sharding import PartitionSpec as P

GROUP = 54
BLOCK = 128
TAPS = 12
FRAME = 768
COLS = FRAME // 128
LOCAL = 27
EDGE = 12
SIGS = 32
KEPT = 64
ROWS = 56

F32 = jnp.float32
BF16 = jnp.bfloat16
NT = (((1,), (1,)), ((), ()))
NN = (((1,), (0,)), ((), ()))


def vmem():
    return pl.BlockSpec(memory_space=pltpu.VMEM)


def anywhere():
    return pl.BlockSpec(memory_space=pl.ANY)


def smem():
    return pl.BlockSpec(memory_space=pltpu.SMEM)


def split(value):
    high = value.astype(BF16)
    return high, (value - high.astype(F32)).astype(BF16)


def fetch(x_ref, buf, sems, col, first, count):
    stations = buf.shape[2]
    return [
        pltpu.make_async_copy(
            x_ref.at[s, pl.ds(first, count), col], buf.at[col, :, s], sems.at[col, s]
        )
        for s in range(stations)
    ]


def coarse_table(kept_ref, w_ref):
    kept = jnp.broadcast_to(kept_ref[...], (KEPT, 128))
    lane = lax.broadcasted_iota(jnp.int32, (KEPT, 128), 1)

    def turn(phase):
        whole = jnp.floor(phase.astype(F32) * (1.0 / FRAME)).astype(jnp.int32)
        angle = (phase - whole * FRAME).astype(F32) * (2.0 * math.pi / FRAME)
        return jnp.cos(angle), -jnp.sin(angle)

    re, im = turn(kept * lane)
    factor = 1.0 / math.sqrt(FRAME)
    re, im = re * factor, im * factor
    step_re, step_im = turn(kept * 128)
    for col in range(COLS):
        span = slice(col * 128, col * 128 + 128)
        for part, value in enumerate((re, im)):
            high, low = split(value)
            w_ref[part * KEPT : part * KEPT + KEPT, span] = high
            w_ref[128 + part * KEPT : 128 + part * KEPT + KEPT, span] = low
        re, im = re * step_re - im * step_im, re * step_im + im * step_re


def filter_column(load, proto_ref, high_ref, low_ref, col, half, sources, outputs):
    lanes = pl.ds(pl.multiple_of(col * 128, 128), 128)
    taps = [jnp.broadcast_to(proto_ref[k : k + 1, lanes], (16, 128)) for k in range(TAPS)]
    sums, left = {}, {}
    for n in sources:
        for k in range(TAPS):
            if (k, n) in outputs:
                left[outputs[k, n]] = left.get(outputs[k, n], 0) + 1
    for n in sources:
        x = load(n, col, half).astype(F32)
        for k in range(TAPS):
            if (k, n) not in outputs:
                continue
            out = outputs[k, n]
            sums[out] = sums[out] + taps[k] * x if out in sums else taps[k] * x
            left[out] -= 1
            if left[out] == 0:
                high, low = split(sums.pop(out))
                rows = pl.ds(pl.multiple_of(out * SIGS + half * 16, 16), 16)
                high_ref[rows, lanes] = high
                low_ref[rows, lanes] = low


def run_filter(x_ref, buf, sems, proto_ref, high_ref, low_ref, first, count, outputs):
    copies = [fetch(x_ref, buf, sems, col, first, count) for col in range(COLS)]
    for group in copies:
        for copy in group:
            copy.start()
    view = buf.reshape(COLS, count, SIGS, 128)

    def load(n, col, half):
        return view[col, n, pl.ds(pl.multiple_of(half * 16, 16), 16), :]

    for col in range(COLS):
        for copy in copies[col]:
            copy.wait()

        @pl.loop(0, 2)
        def _(half):
            filter_column(load, proto_ref, high_ref, low_ref, col, half, range(count), outputs)


def spectrum(w_ref, high_ref, low_ref, first, count):
    rows = slice(first, first + count)
    both = lax.dot_general(w_ref[...], high_ref[rows, :], NT, preferred_element_type=F32)
    rest = lax.dot_general(w_ref[:128, :], low_ref[rows, :], NT, preferred_element_type=F32)
    return both[:128] + both[128:] + rest


def beam_and_deal(load, jones_ref, dealt_ref, tiles, tile_at, stride):
    lane = lax.broadcasted_iota(jnp.int32, (8, 128), 1)
    even = lane % 2 == 0
    low_half = lane < 64
    even_chunk = (lane // 32) % 2 == 0

    def swap(value):
        return jnp.where(even, pltpu.roll(value, 127, 1), pltpu.roll(value, 1, 1))

    def beam(tile, row):
        re, im = load(row, tile), load(KEPT + row, tile)
        swap_re, swap_im = swap(re), swap(im)
        own_re, own_im, cross_re, cross_im = (
            jones_ref[n * KEPT + row : n * KEPT + row + 8, :] for n in range(4)
        )
        return (
            own_re * re - own_im * im + cross_re * swap_re - cross_im * swap_im,
            own_re * im + own_im * re + cross_re * swap_im + cross_im * swap_re,
        )

    for tile in range(tiles):
        for h in range(2):
            beams = [beam(tile, (j * 2 + h) * 8) for j in range(4)]
            for part in range(2):
                v = [beams[j][part] for j in range(4)]
                u = [None] * 4
                for j in range(2):
                    u[j] = jnp.where(low_half, v[j], pltpu.roll(v[j + 2], 64, 1))
                    u[j + 2] = jnp.where(low_half, pltpu.roll(v[j], 64, 1), v[j + 2])
                for i in (0, 2):
                    first = jnp.where(even_chunk, u[i], pltpu.roll(u[i + 1], 32, 1))
                    second = jnp.where(even_chunk, pltpu.roll(u[i], 96, 1), u[i + 1])
                    for n, value in enumerate((first, second)):
                        frame = (tile_at + tile) * 4 + i + n
                        row = h * (stride // 2) + (frame - tile_at * 4) * 2 + part
                        dealt_ref[pl.ds(row, 8, stride=stride), :] = value


MAIN_OUT = {
    (k, n): n + TAPS - 1 - k
    for n in range(LOCAL)
    for k in range(TAPS)
    if n + TAPS - 1 - k < LOCAL
}


def halo_outputs():
    return {(k, f + k): f for f in range(11) for k in range(TAPS) if f + k <= 10}


def halo_kernel(x_ref, proto_ref, kept_ref, w_ref, out_ref, buf, sems, high_ref, low_ref):
    coarse_table(kept_ref, w_ref)
    zero = jnp.zeros((SIGS, FRAME), BF16)
    high_ref[11 * SIGS :, :] = zero
    low_ref[11 * SIGS :, :] = zero
    run_filter(
        x_ref, buf, sems, proto_ref, high_ref, low_ref, LOCAL - 11, 11, halo_outputs()
    )
    out_ref[...] = spectrum(w_ref, high_ref, low_ref, 0, EDGE * SIGS)


def main_kernel(
    x_ref, proto_ref, w_ref, beam_ref, edge_ref, jones_ref, out_ref,
    buf, sems, high_ref, low_ref, coarse_ref, dealt_ref, turned_ref,
):
    side = lax.broadcasted_iota(jnp.int32, (KEPT, 128), 1) % 2 == 0
    for part in range(2):
        for q in range(2):
            rows = beam_ref[pl.ds(q * 2 + part, SIGS, stride=4), :]
            wide = jnp.concatenate([rows.T] * 4, axis=1)
            turned_ref[q * KEPT : q * KEPT + KEPT, :] = wide
        for j in range(4):
            for h in range(2):
                first = turned_ref[pl.ds(4 * h + j, 8, stride=8), :]
                second = turned_ref[pl.ds(KEPT + 4 * h + j, 8, stride=8), :]
                row = (j * 2 + h) * 8
                own = jnp.where(side[:8], first, second)
                cross = jnp.where(side[:8], second, first)
                jones_ref[part * KEPT + row : part * KEPT + row + 8, :] = own
                jones_ref[(2 + part) * KEPT + row : (2 + part) * KEPT + row + 8, :] = cross
    zero = jnp.zeros((SIGS, FRAME), BF16)
    high_ref[LOCAL * SIGS :, :] = zero
    low_ref[LOCAL * SIGS :, :] = zero
    run_filter(x_ref, buf, sems, proto_ref, high_ref, low_ref, 0, LOCAL, MAIN_OUT)
    edge_ref[...] = spectrum(w_ref, high_ref, low_ref, 0, EDGE * SIGS)
    coarse_ref[...] = spectrum(w_ref, high_ref, low_ref, EDGE * SIGS, (LOCAL + 1 - EDGE) * SIGS)
    beam_and_deal(
        lambda row, tile: coarse_ref[row : row + 8, tile * 128 : tile * 128 + 128],
        jones_ref, dealt_ref, 4, 3, 64,
    )
    for d in range(8):
        for h in range(2):
            out_ref[d, h] = dealt_ref[d * 64 + h * 32 : d * 64 + h * 32 + 32, :].astype(BF16)


def edge_kernel(halo_ref, edge_ref, jones_ref, rest_ref, out_ref, dealt_ref):
    def load(row, tile):
        span = slice(tile * 128, tile * 128 + 128)
        return halo_ref[row : row + 8, span] + edge_ref[row : row + 8, span]

    beam_and_deal(load, jones_ref, dealt_ref, 3, 0, 48)
    for d in range(8):
        for h in range(2):
            out_ref[d, h, 0:24, :] = dealt_ref[d * 48 + h * 24 : d * 48 + h * 24 + 24, :].astype(BF16)
            out_ref[d, h, 24:56, :] = rest_ref[d, h]


def fine_table():
    blocks, frames = 8, LOCAL
    length = blocks * frames
    k = np.arange(length)
    angle = 2.0 * np.pi * ((k[:, None] * k[None, :]) % length) / length
    cosine = np.cos(angle) / np.sqrt(length)
    sine = np.sin(angle) / np.sqrt(length)
    groups = length // GROUP
    table = np.zeros((blocks, ROWS, groups, 128))
    view = table[:, : 2 * frames].reshape(blocks, frames, 2, groups, 128)
    cosine = cosine.reshape(blocks, frames, groups, GROUP)
    sine = sine.reshape(blocks, frames, groups, GROUP)
    view[:, :, 0, :, :GROUP] = cosine
    view[:, :, 1, :, :GROUP] = sine
    view[:, :, 0, :, GROUP : 2 * GROUP] = -sine
    view[:, :, 1, :, GROUP : 2 * GROUP] = cosine
    table[:, : 2 * frames] = view.reshape(blocks, 2 * frames, groups, 128)
    table = table.reshape(blocks * ROWS, groups * 128).astype(np.float32)
    high = table.astype(jnp.bfloat16)
    low = (table - high.astype(np.float32)).astype(jnp.bfloat16)
    return np.stack([high, low])


def fine_kernel(x_ref, table_ref, out_ref):
    for h in range(2):
        rows = x_ref[:, h].astype(F32).reshape(8 * ROWS, 128)
        turned = rows.T.astype(BF16)
        fine = lax.dot_general(turned, table_ref[0], NN, preferred_element_type=F32)
        fine = fine + lax.dot_general(turned, table_ref[1], NN, preferred_element_type=F32)
        for j in range(4):
            for g in range(4):
                piece = fine[j * 32 : j * 32 + 32, g * 128 : g * 128 + 128]
                out_ref[(h * 4 + j) * 4 + g] = piece.astype(BF16)


PER_STEP = 4


def pairs_kernel(map_ref, pairs_ref, x_ref, out_ref, ordered_ref, turned_ref):
    step = pl.program_id(0)
    rows = ordered_ref.reshape(1024, 128)

    @pl.when(step == 0)
    def _():
        @pl.loop(0, 512, unroll=8)
        def _(row):
            ordered_ref[map_ref[row]] = x_ref[row]

        lane = lax.broadcasted_iota(jnp.int32, (128, 128), 1)
        for block in range(8):
            value = rows[block * 128 : block * 128 + 128, :].astype(F32)
            turned = jnp.where(
                lane < GROUP, -pltpu.roll(value, 128 - GROUP, 1), pltpu.roll(value, GROUP, 1)
            )
            turned_ref[block * 128 : block * 128 + 128, :] = turned.astype(BF16)

    for n in range(PER_STEP):
        left = pl.ds(pl.multiple_of(pairs_ref[2 * (step * PER_STEP + n)] * 128, 128), 128)
        right = pl.ds(pl.multiple_of(pairs_ref[2 * (step * PER_STEP + n) + 1] * 128, 128), 128)
        own = rows[left, :]
        other = jnp.concatenate([rows[right, :], turned_ref[right, :]], axis=0)
        product = lax.dot_general(own, other, NT, preferred_element_type=F32) * (1.0 / GROUP)
        out_ref[0, n, 0] = product[:, :128]
        out_ref[0, n, 1] = product[:, 128:]


def halo_call(x, proto, kept):
    return pl.pallas_call(
        halo_kernel,
        out_shape=(
            jax.ShapeDtypeStruct((256, FRAME), BF16),
            jax.ShapeDtypeStruct((128, EDGE * SIGS), F32),
        ),
        in_specs=[anywhere(), vmem(), vmem()],
        out_specs=(vmem(), vmem()),
        scratch_shapes=[
            pltpu.VMEM((COLS, 11, 16, 2, 128), BF16),
            pltpu.SemaphoreType.DMA((COLS, 16)),
            pltpu.VMEM((EDGE * SIGS, FRAME), BF16),
            pltpu.VMEM((EDGE * SIGS, FRAME), BF16),
        ],
        name="halo",
    )(x, proto, kept)


def main_call(x, proto, table, jones):
    rows = (LOCAL + 1) * SIGS
    return pl.pallas_call(
        main_kernel,
        out_shape=(
            jax.ShapeDtypeStruct((128, EDGE * SIGS), F32),
            jax.ShapeDtypeStruct((4 * KEPT, 128), F32),
            jax.ShapeDtypeStruct((8, 2, 32, 128), BF16),
        ),
        in_specs=[anywhere(), vmem(), vmem(), vmem()],
        out_specs=(vmem(), vmem(), vmem()),
        scratch_shapes=[
            pltpu.VMEM((COLS, LOCAL, 16, 2, 128), BF16),
            pltpu.SemaphoreType.DMA((COLS, 16)),
            pltpu.VMEM((rows, FRAME), BF16),
            pltpu.VMEM((rows, FRAME), BF16),
            pltpu.VMEM((128, rows - EDGE * SIGS), F32),
            pltpu.VMEM((8 * 64, 128), F32),
            pltpu.VMEM((2 * KEPT, 128), F32),
        ],
        cost_estimate=pl.CostEstimate(flops=10**9, bytes_accessed=4 * 10**6, transcendentals=0),
        name="main",
    )(x, proto, table, jones)


def edge_call(halo, edge, jones, rest):
    return pl.pallas_call(
        edge_kernel,
        out_shape=jax.ShapeDtypeStruct((8, 2, ROWS, 128), BF16),
        in_specs=[vmem()] * 4,
        out_specs=vmem(),
        scratch_shapes=[pltpu.VMEM((8 * 48, 128), F32)],
        name="edge",
    )(halo, edge, jones, rest)


def fine_call(turned, table):
    return pl.pallas_call(
        fine_kernel,
        out_shape=jax.ShapeDtypeStruct((32, SIGS, 128), BF16),
        in_specs=[vmem()] * 2,
        out_specs=vmem(),
        name="fine",
    )(turned, table)


def pairs_call(station_map, tile_pairs, rows):
    tiles = tile_pairs.shape[0] // 2
    return pl.pallas_call(
        pairs_kernel,
        grid=(tiles // PER_STEP,),
        out_shape=jax.ShapeDtypeStruct((1, tiles, 2, BLOCK, BLOCK), F32),
        in_specs=[smem(), smem(), vmem()],
        out_specs=pl.BlockSpec((1, PER_STEP, 2, BLOCK, BLOCK), lambda i: (0, i, 0, 0, 0)),
        scratch_shapes=[pltpu.VMEM((512, 2, 128), BF16), pltpu.VMEM((1024, 128), BF16)],
        name="pairs",
    )(station_map, tile_pairs, rows)


def shards(voltages, prototype, kept_channels, beam_jones, station_map, tile_pairs):
    stations = voltages.shape[0]
    x = voltages.reshape(stations, 2, LOCAL * COLS, 128).transpose(0, 2, 1, 3)
    x = x.reshape(stations, LOCAL, COLS, 2, 128)
    kept = kept_channels.reshape(8, 2, 4).transpose(2, 1, 0).reshape(KEPT, 1)
    table, halo = halo_call(x, prototype, kept)
    blocks = lax.axis_size("tm")
    halo = lax.ppermute(halo, "tm", [(n, n + 1) for n in range(blocks - 1)])
    edge, jones, rest = main_call(x, prototype, table, beam_jones.reshape(128, KEPT))
    beamed = edge_call(halo, edge, jones, rest)
    turned = lax.all_to_all(beamed, "tm", 0, 0, tiled=True)
    fine = fine_call(turned, jnp.asarray(fine_table()))
    fine = fine.reshape(32, 16, 2, 128)
    rows = lax.all_to_all(fine, "stn", 0, 0, tiled=True)
    return pairs_call(station_map, tile_pairs.reshape(-1), rows.reshape(512, 2, 128))


def solution(mesh):
    placed = (P("stn", None, "tm"), P(), P(), P("stn", None, None, None, None), P(), P())
    return jax.shard_map(
        shards,
        mesh=mesh,
        in_specs=placed,
        out_specs=P(("tm", "stn"), None, None, None, None),
        check_vma=False,
    )
```

```python
import functools
import math

import jax
import jax.numpy as jnp
import numpy as np
from jax import lax
from jax.experimental import pallas as pl
from jax.experimental.pallas import tpu as pltpu
from jax.sharding import PartitionSpec as P

GROUP = 54
BLOCK = 128
TAPS = 12
FRAME = 768
COLS = FRAME // 128
LOCAL = 27
EDGE = 12
SIGS = 32
KEPT = 64
ROWS = 56

F32 = jnp.float32
BF16 = jnp.bfloat16
NT = (((1,), (1,)), ((), ()))
NN = (((1,), (0,)), ((), ()))


def vmem():
    return pl.BlockSpec(memory_space=pltpu.VMEM)


def anywhere():
    return pl.BlockSpec(memory_space=pltpu.HBM)


def smem():
    return pl.BlockSpec(memory_space=pltpu.SMEM)


def granted(mebibytes):
    return pltpu.CompilerParams(vmem_limit_bytes=mebibytes * 2**20)


def split(value):
    high = value.astype(BF16)
    return high, (value - high.astype(F32)).astype(BF16)


def turn(phase):
    quarter = jnp.floor((phase + 96.0) * (1.0 / 192.0))
    angle = (phase - quarter * 192.0) * (2.0 * math.pi / FRAME)
    square = angle * angle
    sine = 1.0 / 362880.0
    for term in (-1.0 / 5040.0, 1.0 / 120.0, -1.0 / 6.0, 1.0):
        sine = sine * square + term
    sine = sine * angle
    cosine = 1.0 / 40320.0
    for term in (-1.0 / 720.0, 1.0 / 24.0, -0.5, 1.0):
        cosine = cosine * square + term
    quarter = quarter.astype(jnp.int32) & 3
    odd = (quarter & 1) == 1
    first = jnp.where(odd, sine, cosine)
    second = jnp.where(odd, cosine, sine)
    flip = (quarter == 1) | (quarter == 2)
    return jnp.where(flip, -first, first), jnp.where(quarter >= 2, second, -second)


def coarse_table(kept_ref, turned_ref, w_ref):
    turned_ref[...] = jnp.broadcast_to(kept_ref[...].astype(F32), (128, KEPT)).T
    lane = lax.broadcasted_iota(jnp.int32, (8, 128), 1).astype(F32)
    factor = 1.0 / math.sqrt(FRAME)
    for j in range(4):
        for h in range(2):
            kept = turned_ref[pl.ds(4 * h + j, 8, stride=8), :]
            re, im = turn(kept * lane)
            re, im = re * factor, im * factor
            step_re, step_im = turn(kept * 128.0)
            row = (j * 2 + h) * 8
            for col in range(COLS):
                span = slice(col * 128, col * 128 + 128)
                for part, value in enumerate((re, im)):
                    high, low = split(value)
                    w_ref[part * KEPT + row : part * KEPT + row + 8, span] = high
                    w_ref[128 + part * KEPT + row : 128 + part * KEPT + row + 8, span] = low
                re, im = re * step_re - im * step_im, re * step_im + im * step_re


def filter_column(x_ref, proto_ref, high_ref, low_ref, col, half, lane_at, first, count, outputs):
    taken = pl.ds(pl.multiple_of(col * 128, 128), 128)
    put = pl.ds(pl.multiple_of(lane_at * 128, 128), 128)
    side = pl.ds(pl.multiple_of(half * 16, 16), 16)
    taps = [jnp.broadcast_to(proto_ref[k : k + 1, taken], (16, 128)) for k in range(TAPS)]
    sums, left = {}, {}
    for out in outputs.values():
        left[out] = left.get(out, 0) + 1
    for n in range(count):
        x = x_ref[(first + n) * COLS + col, side, :].astype(F32)
        for k in range(TAPS):
            if (k, n) not in outputs:
                continue
            out = outputs[k, n]
            sums[out] = sums[out] + taps[k] * x if out in sums else taps[k] * x
            left[out] -= 1
            if left[out] == 0:
                high, low = split(sums.pop(out))
                rows = pl.ds(pl.multiple_of(out * SIGS + half * 16, 16), 16)
                high_ref[rows, put] = high
                low_ref[rows, put] = low


def coarse_sums(x_ref, proto_ref, w_ref, highs, lows, sums_ref, first, count, outputs, chunk):
    def transform(pair, q):
        rows = pl.ds(pl.multiple_of(q * chunk, chunk), chunk)
        span = slice(pair * 256, pair * 256 + 256)
        both = lax.dot_general(
            w_ref[:, span], highs[pair][rows, :], NT, preferred_element_type=F32
        )
        rest = lax.dot_general(
            w_ref[:128, span], lows[pair][rows, :], NT, preferred_element_type=F32
        )
        value = both[:128] + both[128:] + rest
        if pair > 0:
            value = value + sums_ref[:, rows]
        sums_ref[:, rows] = value

    for pair in range(COLS // 2):

        @pl.loop(0, 4)
        def _(q):
            if pair > 0:
                transform(pair - 1, q)
            filter_column(
                x_ref, proto_ref, highs[pair], lows[pair],
                pair * 2 + q // 2, q % 2, q // 2, first, count, outputs,
            )

    for q in range(4):
        transform(COLS // 2 - 1, q)


def beam_and_deal(load, jones_ref, dealt_ref, tiles, tile_at, stride):
    lane = lax.broadcasted_iota(jnp.int32, (8, 128), 1)
    even = lane % 2 == 0
    low_half = lane < 64
    even_chunk = (lane // 32) % 2 == 0

    def swap(value):
        return jnp.where(even, pltpu.roll(value, 127, 1), pltpu.roll(value, 1, 1))

    def beam(tile, row):
        re, im = load(row, tile), load(KEPT + row, tile)
        swap_re, swap_im = swap(re), swap(im)
        own_re, own_im, cross_re, cross_im = (
            jones_ref[n * KEPT + row : n * KEPT + row + 8, :] for n in range(4)
        )
        return (
            own_re * re - own_im * im + cross_re * swap_re - cross_im * swap_im,
            own_re * im + own_im * re + cross_re * swap_im + cross_im * swap_re,
        )

    for tile in range(tiles):
        for h in range(2):
            beams = [beam(tile, (j * 2 + h) * 8) for j in range(4)]
            for part in range(2):
                v = [beams[j][part] for j in range(4)]
                u = [None] * 4
                for j in range(2):
                    u[j] = jnp.where(low_half, v[j], pltpu.roll(v[j + 2], 64, 1))
                    u[j + 2] = jnp.where(low_half, pltpu.roll(v[j], 64, 1), v[j + 2])
                for i in (0, 2):
                    first = jnp.where(even_chunk, u[i], pltpu.roll(u[i + 1], 32, 1))
                    second = jnp.where(even_chunk, pltpu.roll(u[i], 96, 1), u[i + 1])
                    for n, value in enumerate((first, second)):
                        frame = (tile_at + tile) * 4 + i + n
                        row = h * (stride // 2) + (frame - tile_at * 4) * 2 + part
                        dealt_ref[pl.ds(row, 8, stride=stride), :] = value


MAIN_OUT = {
    (k, n): n + TAPS - 1 - k
    for n in range(LOCAL)
    for k in range(TAPS)
    if n + TAPS - 1 - k < LOCAL
}


def halo_outputs():
    return {(k, f + k): f for f in range(11) for k in range(TAPS) if f + k <= 10}


def clear(refs, first):
    for ref in refs:
        ref[first : first + SIGS, :] = jnp.zeros((SIGS, 256), BF16)


def halo_kernel(
    x_ref, proto_in, kept_in, beam_in, w_ref, out_ref, xt_ref, proto_ref, beam_ref,
    kept_ref, turned_ref, sums_ref, h0, h1, h2, l0, l1, l2, sems, more,
):
    def rows_of(s, first, count, sem):
        tiles = pl.ds(first * COLS, count * COLS)
        return pltpu.make_async_copy(x_ref.at[s, tiles], xt_ref.at[tiles, pl.ds(2 * s, 2)], sem)

    stations = x_ref.shape[0]
    late = [rows_of(s, LOCAL - 11, 11, sems.at[0, s]) for s in range(stations)]
    early = [rows_of(s, 0, LOCAL - 11, sems.at[1, s]) for s in range(stations)]
    kept_copy = pltpu.make_async_copy(kept_in, kept_ref, more.at[0])
    proto_copy = pltpu.make_async_copy(proto_in, proto_ref, more.at[1])
    beam_copy = pltpu.make_async_copy(beam_in, beam_ref, more.at[2])
    for copy in [kept_copy, proto_copy] + late + early + [beam_copy]:
        copy.start()
    clear((h0, h1, h2, l0, l1, l2), 11 * SIGS)
    kept_copy.wait()
    coarse_table(kept_ref, turned_ref, w_ref)
    for copy in [proto_copy] + late:
        copy.wait()
    coarse_sums(
        xt_ref, proto_ref, w_ref, (h0, h1, h2), (l0, l1, l2), sums_ref,
        LOCAL - 11, 11, halo_outputs(), 128,
    )
    out_ref[...] = sums_ref[:, : EDGE * SIGS]
    for copy in early + [beam_copy]:
        copy.wait()


def main_kernel(
    xt_ref, proto_ref, w_ref, beam_ref, sums_ref, jones_ref, out_ref,
    h0, h1, h2, l0, l1, l2, dealt_ref, turned_ref,
):
    side = lax.broadcasted_iota(jnp.int32, (8, 128), 1) % 2 == 0
    for part in range(2):
        for q in range(2):
            rows = beam_ref[pl.ds(q * 2 + part, SIGS, stride=4), :]
            wide = jnp.concatenate([rows.T] * 4, axis=1)
            turned_ref[q * KEPT : q * KEPT + KEPT, :] = wide
        for j in range(4):
            for h in range(2):
                first = turned_ref[pl.ds(4 * h + j, 8, stride=8), :]
                second = turned_ref[pl.ds(KEPT + 4 * h + j, 8, stride=8), :]
                row = (j * 2 + h) * 8
                own = jnp.where(side, first, second)
                cross = jnp.where(side, second, first)
                jones_ref[part * KEPT + row : part * KEPT + row + 8, :] = own
                jones_ref[(2 + part) * KEPT + row : (2 + part) * KEPT + row + 8, :] = cross
    clear((h0, h1, h2, l0, l1, l2), LOCAL * SIGS)
    coarse_sums(
        xt_ref, proto_ref, w_ref, (h0, h1, h2), (l0, l1, l2), sums_ref,
        0, LOCAL, MAIN_OUT, 256,
    )
    beam_and_deal(
        lambda row, tile: sums_ref[row : row + 8, (3 + tile) * 128 : (3 + tile) * 128 + 128],
        jones_ref, dealt_ref, 4, 3, 64,
    )
    for d in range(8):
        for h in range(2):
            out_ref[d, h] = dealt_ref[d * 64 + h * 32 : d * 64 + h * 32 + 32, :].astype(BF16)


def edge_kernel(halo_ref, edge_ref, jones_ref, rest_ref, out_ref, dealt_ref):
    def load(row, tile):
        span = slice(tile * 128, tile * 128 + 128)
        return halo_ref[row : row + 8, span] + edge_ref[row : row + 8, span]

    beam_and_deal(load, jones_ref, dealt_ref, 3, 0, 48)
    for d in range(8):
        for h in range(2):
            out_ref[d, h, 0:24, :] = dealt_ref[d * 48 + h * 24 : d * 48 + h * 24 + 24, :].astype(BF16)
            out_ref[d, h, 24:56, :] = rest_ref[d, h]


def fine_table():
    blocks, frames = 8, LOCAL
    length = blocks * frames
    k = np.arange(length)
    angle = 2.0 * np.pi * ((k[:, None] * k[None, :]) % length) / length
    cosine = np.cos(angle) / np.sqrt(length)
    sine = np.sin(angle) / np.sqrt(length)
    groups = length // GROUP
    table = np.zeros((blocks, ROWS, groups, 128))
    view = table[:, : 2 * frames].reshape(blocks, frames, 2, groups, 128)
    cosine = cosine.reshape(blocks, frames, groups, GROUP)
    sine = sine.reshape(blocks, frames, groups, GROUP)
    view[:, :, 0, :, :GROUP] = cosine
    view[:, :, 1, :, :GROUP] = sine
    view[:, :, 0, :, GROUP : 2 * GROUP] = -sine
    view[:, :, 1, :, GROUP : 2 * GROUP] = cosine
    table[:, : 2 * frames] = view.reshape(blocks, 2 * frames, groups, 128)
    table = table.reshape(blocks * ROWS, groups * 128).astype(np.float32)
    high = table.astype(jnp.bfloat16)
    low = (table - high.astype(np.float32)).astype(jnp.bfloat16)
    return np.stack([high, low])


def fine_kernel(x_ref, table_ref, out_ref):
    for h in range(2):
        rows = x_ref[:, h].astype(F32).reshape(8 * ROWS, 128)
        turned = rows.T.astype(BF16)
        fine = lax.dot_general(turned, table_ref[0], NN, preferred_element_type=F32)
        fine = fine + lax.dot_general(turned, table_ref[1], NN, preferred_element_type=F32)
        for j in range(4):
            for g in range(4):
                piece = fine[j * 32 : j * 32 + 32, g * 128 : g * 128 + 128]
                out_ref[(h * 4 + j) * 4 + g] = piece.astype(BF16)


def pairs_kernel(map_ref, pairs_ref, x_ref, out_ref, ordered_ref, own_ref, turned_ref, made, sems):
    tiles = made.shape[0]
    rows = ordered_ref.reshape(1024, 128)

    @pl.loop(0, 512, unroll=8)
    def _(row):
        ordered_ref[map_ref[row]] = x_ref[row]

    lane = lax.broadcasted_iota(jnp.int32, (128, 128), 1)
    for block in range(8):
        span = slice(block * 128, block * 128 + 128)
        own = rows[span, :]
        own_ref[span, :] = own
        value = own.astype(F32)
        turned = jnp.where(
            lane < GROUP, -pltpu.roll(value, 128 - GROUP, 1), pltpu.roll(value, GROUP, 1)
        )
        turned_ref[span, :] = turned.astype(BF16)

    def send(tile):
        return pltpu.make_async_copy(made.at[tile], out_ref.at[0, tile], sems.at[tile])

    @pl.loop(0, tiles, unroll=12)
    def _(tile):
        left = pl.ds(pl.multiple_of(pairs_ref[0, tile] * 128, 128), 128)
        right = pl.ds(pl.multiple_of(pairs_ref[1, tile] * 128, 128), 128)
        other = jnp.concatenate([own_ref[right, :], turned_ref[right, :]], axis=0)
        product = lax.dot_general(own_ref[left, :], other, NT, preferred_element_type=F32)
        product = product * (1.0 / GROUP)
        made[tile, 0] = product[:, :128]
        made[tile, 1] = product[:, 128:]
        send(tile).start()

    @pl.loop(0, tiles)
    def _(tile):
        send(tile).wait()


def columns(rows):
    return [pltpu.VMEM((rows, 256), BF16)] * 6


def halo_call(x, proto, kept, beam):
    return pl.pallas_call(
        halo_kernel,
        out_shape=(
            jax.ShapeDtypeStruct((256, FRAME), BF16),
            jax.ShapeDtypeStruct((128, EDGE * SIGS), F32),
            jax.ShapeDtypeStruct((LOCAL * COLS, SIGS, 128), BF16),
            jax.ShapeDtypeStruct(proto.shape, F32),
            jax.ShapeDtypeStruct(beam.shape, F32),
        ),
        in_specs=[anywhere()] * 4,
        out_specs=(vmem(),) * 5,
        scratch_shapes=[
            pltpu.VMEM((1, KEPT), jnp.int32),
            pltpu.VMEM((KEPT, 128), F32),
            pltpu.VMEM((128, 512), F32),
            *columns(512),
            pltpu.SemaphoreType.DMA((2, 16)),
            pltpu.SemaphoreType.DMA((3,)),
        ],
        compiler_params=granted(8),
        name="halo",
    )(x, proto, kept, beam)


def main_call(xt, proto, table, beam):
    return pl.pallas_call(
        main_kernel,
        out_shape=(
            jax.ShapeDtypeStruct((128, 1024), F32),
            jax.ShapeDtypeStruct((4 * KEPT, 128), F32),
            jax.ShapeDtypeStruct((8, 2, 32, 128), BF16),
        ),
        in_specs=[vmem()] * 4,
        out_specs=(vmem(),) * 3,
        scratch_shapes=[
            *columns(1024),
            pltpu.VMEM((8 * 64, 128), F32),
            pltpu.VMEM((2 * KEPT, 128), F32),
        ],
        compiler_params=granted(14),
        cost_estimate=pl.CostEstimate(flops=10**9, bytes_accessed=4 * 10**6, transcendentals=0),
        name="main",
    )(xt, proto, table, beam)


def edge_call(halo, edge, jones, rest):
    return pl.pallas_call(
        edge_kernel,
        out_shape=jax.ShapeDtypeStruct((8, 2, ROWS, 128), BF16),
        in_specs=[vmem()] * 4,
        out_specs=vmem(),
        scratch_shapes=[pltpu.VMEM((8 * 48, 128), F32)],
        compiler_params=granted(4),
        name="edge",
    )(halo, edge, jones, rest)


def fine_call(turned, table):
    return pl.pallas_call(
        fine_kernel,
        out_shape=jax.ShapeDtypeStruct((32, SIGS, 128), BF16),
        in_specs=[vmem()] * 2,
        out_specs=vmem(),
        compiler_params=granted(8),
        name="fine",
    )(turned, table)


def pairs_call(station_map, tile_pairs, rows):
    tiles = tile_pairs.shape[1]
    return pl.pallas_call(
        pairs_kernel,
        out_shape=jax.ShapeDtypeStruct((1, tiles, 2, BLOCK, BLOCK), F32),
        in_specs=[smem(), smem(), vmem()],
        out_specs=anywhere(),
        scratch_shapes=[
            pltpu.VMEM((512, 2, 128), BF16),
            pltpu.VMEM((1024, 128), BF16),
            pltpu.VMEM((1024, 128), BF16),
            pltpu.VMEM((tiles, 2, BLOCK, BLOCK), F32),
            pltpu.SemaphoreType.DMA((tiles,)),
        ],
        compiler_params=granted(10),
        name="pairs",
    )(station_map, tile_pairs, rows)


def kept_in_hbm(value):
    return pltpu.with_memory_space_constraint(value, pltpu.HBM)


def shards(voltages, prototype, kept_channels, beam_jones, station_map, tile_pairs):
    stations = voltages.shape[0]
    x = voltages.reshape(stations, 2, LOCAL * COLS, 128).transpose(0, 2, 1, 3)
    table, halo, xt, proto, beam = halo_call(
        kept_in_hbm(x),
        kept_in_hbm(prototype),
        kept_in_hbm(kept_channels.reshape(1, KEPT)),
        kept_in_hbm(beam_jones.reshape(128, KEPT)),
    )
    blocks = lax.axis_size("tm")
    halo = lax.ppermute(halo, "tm", [(n, n + 1) for n in range(blocks - 1)])
    sums, jones, rest = main_call(xt, proto, table, beam)
    beamed = edge_call(halo, sums, jones, rest)
    turned = lax.all_to_all(beamed, "tm", 0, 0, tiled=True)
    fine = fine_call(turned, jnp.asarray(fine_table()))
    fine = fine.reshape(32, 16, 2, 128)
    rows = lax.all_to_all(fine, "stn", 0, 0, tiled=True)
    return pairs_call(station_map, tile_pairs.T, rows.reshape(512, 2, 128))


def solution(mesh):
    placed = (P("stn", None, "tm"), P(), P(), P("stn", None, None, None, None), P(), P())
    return jax.shard_map(
        shards,
        mesh=mesh,
        in_specs=placed,
        out_specs=P(("tm", "stn"), None, None, None, None),
        check_vma=False,
    )
```

```python
import functools
import math

import jax
import jax.numpy as jnp
import numpy as np
from jax import lax
from jax.experimental import pallas as pl
from jax.experimental.pallas import tpu as pltpu
from jax.sharding import PartitionSpec as P

GROUP = 54
BLOCK = 128
TAPS = 12
FRAME = 768
COLS = FRAME // 128
LOCAL = 27
SPREAD = LOCAL + TAPS - 1
TILES = 10
STEPS = 5
SIGS = 32
KEPT = 64
ROWS = 80

F32 = jnp.float32
BF16 = jnp.bfloat16
NT = (((1,), (1,)), ((), ()))
NN = (((1,), (0,)), ((), ()))


def vmem():
    return pl.BlockSpec(memory_space=pltpu.VMEM)


def anywhere():
    return pl.BlockSpec(memory_space=pltpu.HBM)


def smem():
    return pl.BlockSpec(memory_space=pltpu.SMEM)


def granted(mebibytes):
    return pltpu.CompilerParams(vmem_limit_bytes=mebibytes * 2**20)


def split(value):
    high = value.astype(BF16)
    return high, (value - high.astype(F32)).astype(BF16)


def turn(phase):
    quarter = jnp.floor((phase + 96.0) * (1.0 / 192.0))
    angle = (phase - quarter * 192.0) * (2.0 * math.pi / FRAME)
    square = angle * angle
    sine = 1.0 / 362880.0
    for term in (-1.0 / 5040.0, 1.0 / 120.0, -1.0 / 6.0, 1.0):
        sine = sine * square + term
    sine = sine * angle
    cosine = 1.0 / 40320.0
    for term in (-1.0 / 720.0, 1.0 / 24.0, -0.5, 1.0):
        cosine = cosine * square + term
    quarter = quarter.astype(jnp.int32) & 3
    odd = (quarter & 1) == 1
    first = jnp.where(odd, sine, cosine)
    second = jnp.where(odd, cosine, sine)
    flip = (quarter == 1) | (quarter == 2)
    return jnp.where(flip, -first, first), jnp.where(quarter >= 2, second, -second)


def coarse_table(kept_ref, turned_ref, w_ref):
    turned_ref[:KEPT, :] = jnp.broadcast_to(kept_ref[...].astype(F32), (128, KEPT)).T
    lane = lax.broadcasted_iota(jnp.int32, (8, 128), 1).astype(F32)
    factor = 1.0 / math.sqrt(FRAME)
    for j in range(4):
        for h in range(2):
            kept = turned_ref[pl.ds(4 * h + j, 8, stride=8), :]
            re, im = turn(kept * lane)
            re, im = re * factor, im * factor
            step_re, step_im = turn(kept * 128.0)
            row = (j * 2 + h) * 8
            for col in range(COLS):
                span = slice(col * 128, col * 128 + 128)
                for part, value in enumerate((re, im)):
                    high, low = split(value)
                    w_ref[part * KEPT + row : part * KEPT + row + 8, span] = high
                    w_ref[128 + part * KEPT + row : 128 + part * KEPT + row + 8, span] = low
                re, im = re * step_re - im * step_im, re * step_im + im * step_re


def filter_column(x_ref, proto_ref, high_ref, low_ref, col, half, lane_at, outputs):
    taken = pl.ds(pl.multiple_of(col * 128, 128), 128)
    put = pl.ds(pl.multiple_of(lane_at * 128, 128), 128)
    side = pl.ds(pl.multiple_of(half * 16, 16), 16)
    taps = [jnp.broadcast_to(proto_ref[k : k + 1, taken], (16, 128)) for k in range(TAPS)]
    sums, left = {}, {}
    for out in outputs.values():
        left[out] = left.get(out, 0) + 1
    for n in range(LOCAL):
        x = x_ref[n * COLS + col, side, :].astype(F32)
        for k in range(TAPS):
            if (k, n) not in outputs:
                continue
            out = outputs[k, n]
            sums[out] = sums[out] + taps[k] * x if out in sums else taps[k] * x
            left[out] -= 1
            if left[out] == 0:
                high, low = split(sums.pop(out))
                rows = pl.ds(pl.multiple_of(out * SIGS + half * 16, 16), 16)
                high_ref[rows, put] = high
                low_ref[rows, put] = low


def coarse_sums(x_ref, proto_ref, w_ref, highs, lows, sums_ref, outputs):
    chunk = TILES * 128 // STEPS

    def transform(pair, q):
        rows = pl.ds(pl.multiple_of(q * chunk, chunk), chunk)
        span = slice(pair * 256, pair * 256 + 256)
        both = lax.dot_general(
            w_ref[:, span], highs[pair][rows, :], NT, preferred_element_type=F32
        )
        rest = lax.dot_general(
            w_ref[:128, span], lows[pair][rows, :], NT, preferred_element_type=F32
        )
        value = both[:128] + both[128:] + rest
        if pair > 0:
            value = value + sums_ref[:, rows]
        sums_ref[:, rows] = value

    for pair in range(COLS // 2):

        if pair > 0:
            transform(pair - 1, STEPS - 1)

        @pl.loop(0, 4)
        def _(q):
            if pair > 0:
                transform(pair - 1, q)
            filter_column(
                x_ref, proto_ref, highs[pair], lows[pair],
                pair * 2 + q // 2, q % 2, q // 2, outputs,
            )

    for q in range(STEPS):
        transform(COLS // 2 - 1, q)


def beam_and_deal(load, jones_ref, dealt_ref, tiles, stride):
    lane = lax.broadcasted_iota(jnp.int32, (8, 128), 1)
    even = lane % 2 == 0
    low_half = lane < 64
    even_chunk = (lane // 32) % 2 == 0

    def swap(value):
        return jnp.where(even, pltpu.roll(value, 127, 1), pltpu.roll(value, 1, 1))

    def beam(tile, row):
        re, im = load(row, tile), load(KEPT + row, tile)
        swap_re, swap_im = swap(re), swap(im)
        own_re, own_im, cross_re, cross_im = (
            jones_ref[n * KEPT + row : n * KEPT + row + 8, :] for n in range(4)
        )
        return (
            own_re * re - own_im * im + cross_re * swap_re - cross_im * swap_im,
            own_re * im + own_im * re + cross_re * swap_im + cross_im * swap_re,
        )

    for tile in range(tiles):
        for h in range(2):
            beams = [beam(tile, (j * 2 + h) * 8) for j in range(4)]
            for part in range(2):
                v = [beams[j][part] for j in range(4)]
                u = [None] * 4
                for j in range(2):
                    u[j] = jnp.where(low_half, v[j], pltpu.roll(v[j + 2], 64, 1))
                    u[j + 2] = jnp.where(low_half, pltpu.roll(v[j], 64, 1), v[j + 2])
                for i in (0, 2):
                    first = jnp.where(even_chunk, u[i], pltpu.roll(u[i + 1], 32, 1))
                    second = jnp.where(even_chunk, pltpu.roll(u[i], 96, 1), u[i + 1])
                    for n, value in enumerate((first, second)):
                        row = h * (stride // 2) + (tile * 4 + i + n) * 2 + part
                        dealt_ref[pl.ds(row, 8, stride=stride), :] = value


MAIN_OUT = {
    (k, n): n + TAPS - 1 - k
    for n in range(LOCAL)
    for k in range(TAPS)
    if n + TAPS - 1 - k < LOCAL
}


def clear(refs, first, last):
    for ref in refs:
        ref[first:last, :] = jnp.zeros((last - first, 256), BF16)


def deal_beam(beam_ref, turned_ref, jones_ref):
    side = lax.broadcasted_iota(jnp.int32, (8, 128), 1) % 2 == 0
    for part in range(2):
        for q in range(2):
            rows = beam_ref[pl.ds(q * 2 + part, SIGS, stride=4), :]
            wide = jnp.concatenate([rows.T] * 4, axis=1)
            turned_ref[q * KEPT : q * KEPT + KEPT, :] = wide
        for j in range(4):
            for h in range(2):
                first = turned_ref[pl.ds(4 * h + j, 8, stride=8), :]
                second = turned_ref[pl.ds(KEPT + 4 * h + j, 8, stride=8), :]
                row = (j * 2 + h) * 8
                own = jnp.where(side, first, second)
                cross = jnp.where(side, second, first)
                jones_ref[part * KEPT + row : part * KEPT + row + 8, :] = own
                jones_ref[(2 + part) * KEPT + row : (2 + part) * KEPT + row + 8, :] = cross


def front_kernel(
    x_ref, proto_in, kept_in, beam_in, out_ref, xt_ref, proto_ref, beam_ref, kept_ref,
    w_ref, jones_ref, turned_ref, sums_ref, dealt_ref, h0, h1, h2, l0, l1, l2, sems, more,
):
    stations = x_ref.shape[0]
    rows = [
        pltpu.make_async_copy(x_ref.at[s], xt_ref.at[:, pl.ds(2 * s, 2)], sems.at[s])
        for s in range(stations)
    ]
    kept_copy = pltpu.make_async_copy(kept_in, kept_ref, more.at[0])
    proto_copy = pltpu.make_async_copy(proto_in, proto_ref, more.at[1])
    beam_copy = pltpu.make_async_copy(beam_in, beam_ref, more.at[2])
    for copy in [kept_copy, beam_copy, proto_copy] + rows:
        copy.start()
    clear((h0, h1, h2, l0, l1, l2), SPREAD * SIGS, TILES * 128)
    kept_copy.wait()
    beam_copy.wait()
    coarse_table(kept_ref, turned_ref, w_ref)
    deal_beam(beam_ref, turned_ref, jones_ref)
    for copy in [proto_copy] + rows:
        copy.wait()
    outputs = {(k, n): n + TAPS - 1 - k for n in range(LOCAL) for k in range(TAPS)}
    coarse_sums(
        xt_ref, proto_ref, w_ref, (h0, h1, h2), (l0, l1, l2), sums_ref, outputs,
    )
    beam_and_deal(
        lambda row, tile: sums_ref[row : row + 8, tile * 128 : tile * 128 + 128],
        jones_ref, dealt_ref, TILES, 2 * ROWS,
    )
    for d in range(8):
        for h in range(2):
            first = (d * 2 + h) * ROWS
            out_ref[d, h] = dealt_ref[first : first + ROWS, :].astype(BF16)


def fine_table():
    blocks = 8
    length = blocks * LOCAL
    groups = length // GROUP
    table = np.zeros((blocks, ROWS, groups, 128))
    k = np.arange(length)
    for block in range(blocks):
        for local in range(SPREAD):
            frame = block * LOCAL + local
            if frame >= length:
                continue
            angle = 2.0 * np.pi * ((frame * k) % length) / length
            cosine = (np.cos(angle) / np.sqrt(length)).reshape(groups, GROUP)
            sine = (np.sin(angle) / np.sqrt(length)).reshape(groups, GROUP)
            table[block, 2 * local, :, :GROUP] = cosine
            table[block, 2 * local, :, GROUP : 2 * GROUP] = -sine
            table[block, 2 * local + 1, :, :GROUP] = sine
            table[block, 2 * local + 1, :, GROUP : 2 * GROUP] = cosine
    table = table.reshape(blocks * ROWS, groups * 128).astype(np.float32)
    high = table.astype(jnp.bfloat16)
    low = (table - high.astype(np.float32)).astype(jnp.bfloat16)
    return np.stack([high, low])


def fine_kernel(x_ref, table_ref, out_ref):
    for h in range(2):
        rows = x_ref[:, h].astype(F32).reshape(8 * ROWS, 128)
        turned = rows.T.astype(BF16)
        fine = lax.dot_general(turned, table_ref[0], NN, preferred_element_type=F32)
        fine = fine + lax.dot_general(turned, table_ref[1], NN, preferred_element_type=F32)
        for j in range(4):
            for g in range(4):
                piece = fine[j * 32 : j * 32 + 32, g * 128 : g * 128 + 128]
                out_ref[(h * 4 + j) * 4 + g] = piece.astype(BF16)


def pairs_kernel(map_ref, pairs_ref, x_ref, out_ref, ordered_ref, own_ref, turned_ref, made, sems):
    tiles = made.shape[0]
    rows = ordered_ref.reshape(1024, 128)

    @pl.loop(0, 512, unroll=8)
    def _(row):
        ordered_ref[map_ref[row]] = x_ref[row]

    lane = lax.broadcasted_iota(jnp.int32, (128, 128), 1)
    for block in range(8):
        span = slice(block * 128, block * 128 + 128)
        own = rows[span, :]
        own_ref[span, :] = own
        value = own.astype(F32)
        turned = jnp.where(
            lane < GROUP, -pltpu.roll(value, 128 - GROUP, 1), pltpu.roll(value, GROUP, 1)
        )
        turned_ref[span, :] = turned.astype(BF16)

    def send(tile):
        return pltpu.make_async_copy(made.at[tile], out_ref.at[0, tile], sems.at[tile])

    @pl.loop(0, tiles, unroll=12)
    def _(tile):
        left = pl.ds(pl.multiple_of(pairs_ref[0, tile] * 128, 128), 128)
        right = pl.ds(pl.multiple_of(pairs_ref[1, tile] * 128, 128), 128)
        other = jnp.concatenate([own_ref[right, :], turned_ref[right, :]], axis=0)
        product = lax.dot_general(own_ref[left, :], other, NT, preferred_element_type=F32)
        product = product * (1.0 / GROUP)
        made[tile, 0] = product[:, :128]
        made[tile, 1] = product[:, 128:]
        send(tile).start()

    @pl.loop(0, tiles)
    def _(tile):
        send(tile).wait()


def columns(rows):
    return [pltpu.VMEM((rows, 256), BF16)] * 6


def front_call(x, proto, kept, beam):
    rows = TILES * 128
    return pl.pallas_call(
        front_kernel,
        out_shape=jax.ShapeDtypeStruct((8, 2, ROWS, 128), BF16),
        in_specs=[anywhere()] * 4,
        out_specs=vmem(),
        scratch_shapes=[
            pltpu.VMEM((LOCAL * COLS, SIGS, 128), BF16),
            pltpu.VMEM(proto.shape, F32),
            pltpu.VMEM(beam.shape, F32),
            pltpu.VMEM((1, KEPT), jnp.int32),
            pltpu.VMEM((256, FRAME), BF16),
            pltpu.VMEM((4 * KEPT, 128), F32),
            pltpu.VMEM((2 * KEPT, 128), F32),
            pltpu.VMEM((128, rows), F32),
            pltpu.VMEM((16 * ROWS, 128), F32),
            *[pltpu.VMEM((rows, 256), BF16)] * 6,
            pltpu.SemaphoreType.DMA((16,)),
            pltpu.SemaphoreType.DMA((3,)),
        ],
        compiler_params=granted(16),
        name="front",
    )(x, proto, kept, beam)


def fine_call(turned, table):
    return pl.pallas_call(
        fine_kernel,
        out_shape=jax.ShapeDtypeStruct((32, SIGS, 128), BF16),
        in_specs=[vmem()] * 2,
        out_specs=vmem(),
        compiler_params=granted(8),
        name="fine",
    )(turned, table)


def pairs_call(station_map, tile_pairs, rows):
    tiles = tile_pairs.shape[1]
    return pl.pallas_call(
        pairs_kernel,
        out_shape=jax.ShapeDtypeStruct((1, tiles, 2, BLOCK, BLOCK), F32),
        in_specs=[smem(), smem(), vmem()],
        out_specs=anywhere(),
        scratch_shapes=[
            pltpu.VMEM((512, 2, 128), BF16),
            pltpu.VMEM((1024, 128), BF16),
            pltpu.VMEM((1024, 128), BF16),
            pltpu.VMEM((tiles, 2, BLOCK, BLOCK), F32),
            pltpu.SemaphoreType.DMA((tiles,)),
        ],
        compiler_params=granted(10),
        name="pairs",
    )(station_map, tile_pairs, rows)


def kept_in_hbm(value):
    return pltpu.with_memory_space_constraint(value, pltpu.HBM)


def shards(voltages, prototype, kept_channels, beam_jones, station_map, tile_pairs):
    stations = voltages.shape[0]
    x = voltages.reshape(stations, 2, LOCAL * COLS, 128).transpose(0, 2, 1, 3)
    beamed = front_call(
        kept_in_hbm(x),
        kept_in_hbm(prototype),
        kept_in_hbm(kept_channels.reshape(1, KEPT)),
        kept_in_hbm(beam_jones.reshape(128, KEPT)),
    )
    turned = lax.all_to_all(beamed, "tm", 0, 0, tiled=True)
    fine = fine_call(turned, jnp.asarray(fine_table()))
    fine = fine.reshape(32, 16, 2, 128)
    rows = lax.all_to_all(fine, "stn", 0, 0, tiled=True)
    return pairs_call(station_map, tile_pairs.T, rows.reshape(512, 2, 128))


def solution(mesh):
    placed = (P("stn", None, "tm"), P(), P(), P("stn", None, None, None, None), P(), P())
    return jax.shard_map(
        shards,
        mesh=mesh,
        in_specs=placed,
        out_specs=P(("tm", "stn"), None, None, None, None),
        check_vma=False,
    )
```

```python
import functools
import math

import jax
import jax.numpy as jnp
import numpy as np
from jax import lax
from jax.experimental import pallas as pl
from jax.experimental.pallas import tpu as pltpu
from jax.sharding import PartitionSpec as P

GROUP = 54
BLOCK = 128
TAPS = 12
FRAME = 768
COLS = FRAME // 128
LOCAL = 27
SPREAD = LOCAL + TAPS - 1
TILES = 10
STEPS = 10
PADDED = 1536
SIGS = 32
KEPT = 64
ROWS = 80

F32 = jnp.float32
BF16 = jnp.bfloat16
NT = (((1,), (1,)), ((), ()))
NN = (((1,), (0,)), ((), ()))


def vmem():
    return pl.BlockSpec(memory_space=pltpu.VMEM)


def anywhere():
    return pl.BlockSpec(memory_space=pltpu.HBM)


def smem():
    return pl.BlockSpec(memory_space=pltpu.SMEM)


def granted(mebibytes):
    return pltpu.CompilerParams(vmem_limit_bytes=mebibytes * 2**20)


def split(value):
    high = value.astype(BF16)
    return high, (value - high.astype(F32)).astype(BF16)


def turn(phase):
    quarter = jnp.floor((phase + 96.0) * (1.0 / 192.0))
    angle = (phase - quarter * 192.0) * (2.0 * math.pi / FRAME)
    square = angle * angle
    sine = 1.0 / 362880.0
    for term in (-1.0 / 5040.0, 1.0 / 120.0, -1.0 / 6.0, 1.0):
        sine = sine * square + term
    sine = sine * angle
    cosine = 1.0 / 40320.0
    for term in (-1.0 / 720.0, 1.0 / 24.0, -0.5, 1.0):
        cosine = cosine * square + term
    quarter = quarter.astype(jnp.int32) & 3
    odd = (quarter & 1) == 1
    first = jnp.where(odd, sine, cosine)
    second = jnp.where(odd, cosine, sine)
    flip = (quarter == 1) | (quarter == 2)
    return jnp.where(flip, -first, first), jnp.where(quarter >= 2, second, -second)


def coarse_table(kept_ref, turned_ref, w_ref):
    turned_ref[:KEPT, :] = jnp.broadcast_to(kept_ref[...].astype(F32), (128, KEPT)).T
    lane = lax.broadcasted_iota(jnp.int32, (8, 128), 1).astype(F32)
    factor = 1.0 / math.sqrt(FRAME)
    for j in range(4):
        for h in range(2):
            kept = turned_ref[pl.ds(4 * h + j, 8, stride=8), :]
            re, im = turn(kept * lane)
            re, im = re * factor, im * factor
            step_re, step_im = turn(kept * 128.0)
            row = (j * 2 + h) * 8
            for col in range(COLS):
                span = slice(col * 128, col * 128 + 128)
                for part, value in enumerate((re, im)):
                    high, low = split(value)
                    w_ref[part * KEPT + row : part * KEPT + row + 8, span] = high
                    w_ref[128 + part * KEPT + row : 128 + part * KEPT + row + 8, span] = low
                re, im = re * step_re - im * step_im, re * step_im + im * step_re


def filter_column(x_ref, proto_ref, high_ref, low_ref, col, half, lane_at, outputs):
    taken = pl.ds(pl.multiple_of(col * 128, 128), 128)
    put = pl.ds(pl.multiple_of(lane_at * 128, 128), 128)
    side = pl.ds(pl.multiple_of(half * 16, 16), 16)
    taps = [jnp.broadcast_to(proto_ref[k : k + 1, taken], (16, 128)) for k in range(TAPS)]
    sums, left = {}, {}
    for out in outputs.values():
        left[out] = left.get(out, 0) + 1
    for n in range(LOCAL):
        x = x_ref[n * COLS + col, side, :].astype(F32)
        for k in range(TAPS):
            if (k, n) not in outputs:
                continue
            out = outputs[k, n]
            sums[out] = sums[out] + taps[k] * x if out in sums else taps[k] * x
            left[out] -= 1
            if left[out] == 0:
                high, low = split(sums.pop(out))
                rows = pl.ds(pl.multiple_of(out * SIGS + half * 16, 16), 16)
                high_ref[rows, put] = high
                low_ref[rows, put] = low


def coarse_sums(x_ref, proto_ref, w_ref, highs, lows, sums_ref, outputs):
    def transform(pair, q, chunk):
        rows = pl.ds(pl.multiple_of(q * chunk, chunk), chunk)
        span = slice(pair * 256, pair * 256 + 256)
        both = lax.dot_general(
            w_ref[:, span], highs[pair][rows, :], NT, preferred_element_type=F32
        )
        rest = lax.dot_general(
            w_ref[:128, span], lows[pair][rows, :], NT, preferred_element_type=F32
        )
        value = both[:128] + both[128:] + rest
        if pair > 0:
            value = value + sums_ref[:, rows]
        sums_ref[:, rows] = value

    for pair in range(COLS // 2):

        @pl.loop(0, 4)
        def _(q):
            if pair > 0:
                transform(pair - 1, q, PADDED // 4)
            filter_column(
                x_ref, proto_ref, highs[pair], lows[pair],
                pair * 2 + q // 2, q % 2, q // 2, outputs,
            )

    for q in range(STEPS):
        transform(COLS // 2 - 1, q, TILES * 128 // STEPS)


def beam_and_deal(load, jones_ref, dealt_ref, tiles, stride):
    lane = lax.broadcasted_iota(jnp.int32, (8, 128), 1)
    even = lane % 2 == 0
    low_half = lane < 64
    even_chunk = (lane // 32) % 2 == 0

    def swap(value):
        return jnp.where(even, pltpu.roll(value, 127, 1), pltpu.roll(value, 1, 1))

    def beam(tile, row):
        re, im = load(row, tile), load(KEPT + row, tile)
        swap_re, swap_im = swap(re), swap(im)
        own_re, own_im, cross_re, cross_im = (
            jones_ref[n * KEPT + row : n * KEPT + row + 8, :] for n in range(4)
        )
        return (
            own_re * re - own_im * im + cross_re * swap_re - cross_im * swap_im,
            own_re * im + own_im * re + cross_re * swap_im + cross_im * swap_re,
        )

    for tile in range(tiles):
        for h in range(2):
            beams = [beam(tile, (j * 2 + h) * 8) for j in range(4)]
            for part in range(2):
                v = [beams[j][part] for j in range(4)]
                u = [None] * 4
                for j in range(2):
                    u[j] = jnp.where(low_half, v[j], pltpu.roll(v[j + 2], 64, 1))
                    u[j + 2] = jnp.where(low_half, pltpu.roll(v[j], 64, 1), v[j + 2])
                for i in (0, 2):
                    first = jnp.where(even_chunk, u[i], pltpu.roll(u[i + 1], 32, 1))
                    second = jnp.where(even_chunk, pltpu.roll(u[i], 96, 1), u[i + 1])
                    for n, value in enumerate((first, second)):
                        row = h * (stride // 2) + (tile * 4 + i + n) * 2 + part
                        dealt_ref[pl.ds(row, 8, stride=stride), :] = value


MAIN_OUT = {
    (k, n): n + TAPS - 1 - k
    for n in range(LOCAL)
    for k in range(TAPS)
    if n + TAPS - 1 - k < LOCAL
}


def clear(refs, first, last):
    for ref in refs:
        ref[first:last, :] = jnp.zeros((last - first, 256), BF16)


def deal_beam(beam_ref, turned_ref, jones_ref):
    side = lax.broadcasted_iota(jnp.int32, (8, 128), 1) % 2 == 0
    for part in range(2):
        for q in range(2):
            rows = beam_ref[pl.ds(q * 2 + part, SIGS, stride=4), :]
            wide = jnp.concatenate([rows.T] * 4, axis=1)
            turned_ref[q * KEPT : q * KEPT + KEPT, :] = wide
        for j in range(4):
            for h in range(2):
                first = turned_ref[pl.ds(4 * h + j, 8, stride=8), :]
                second = turned_ref[pl.ds(KEPT + 4 * h + j, 8, stride=8), :]
                row = (j * 2 + h) * 8
                own = jnp.where(side, first, second)
                cross = jnp.where(side, second, first)
                jones_ref[part * KEPT + row : part * KEPT + row + 8, :] = own
                jones_ref[(2 + part) * KEPT + row : (2 + part) * KEPT + row + 8, :] = cross


def front_kernel(
    x_ref, proto_in, kept_in, beam_in, out_ref, xt_ref, proto_ref, beam_ref, kept_ref,
    w_ref, jones_ref, turned_ref, sums_ref, dealt_ref, h0, h1, h2, l0, l1, l2, sems, more,
):
    stations = x_ref.shape[0]
    rows = [
        pltpu.make_async_copy(x_ref.at[s], xt_ref.at[:, pl.ds(2 * s, 2)], sems.at[s])
        for s in range(stations)
    ]
    kept_copy = pltpu.make_async_copy(kept_in, kept_ref, more.at[0])
    proto_copy = pltpu.make_async_copy(proto_in, proto_ref, more.at[1])
    beam_copy = pltpu.make_async_copy(beam_in, beam_ref, more.at[2])
    for copy in [kept_copy, beam_copy, proto_copy] + rows:
        copy.start()
    clear((h0, h1, h2, l0, l1, l2), SPREAD * SIGS, TILES * 128)
    kept_copy.wait()
    beam_copy.wait()
    coarse_table(kept_ref, turned_ref, w_ref)
    deal_beam(beam_ref, turned_ref, jones_ref)
    for copy in [proto_copy] + rows:
        copy.wait()
    outputs = {(k, n): n + TAPS - 1 - k for n in range(LOCAL) for k in range(TAPS)}
    coarse_sums(
        xt_ref, proto_ref, w_ref, (h0, h1, h2), (l0, l1, l2), sums_ref, outputs,
    )
    beam_and_deal(
        lambda row, tile: sums_ref[row : row + 8, tile * 128 : tile * 128 + 128],
        jones_ref, dealt_ref, TILES, 2 * ROWS,
    )
    for d in range(8):
        for h in range(2):
            first = (d * 2 + h) * ROWS
            out_ref[d, h] = dealt_ref[first : first + ROWS, :].astype(BF16)


def fine_table():
    blocks = 8
    length = blocks * LOCAL
    groups = length // GROUP
    table = np.zeros((blocks, ROWS, groups, 128))
    k = np.arange(length)
    for block in range(blocks):
        for local in range(SPREAD):
            frame = block * LOCAL + local
            if frame >= length:
                continue
            angle = 2.0 * np.pi * ((frame * k) % length) / length
            cosine = (np.cos(angle) / np.sqrt(length)).reshape(groups, GROUP)
            sine = (np.sin(angle) / np.sqrt(length)).reshape(groups, GROUP)
            table[block, 2 * local, :, :GROUP] = cosine
            table[block, 2 * local, :, GROUP : 2 * GROUP] = -sine
            table[block, 2 * local + 1, :, :GROUP] = sine
            table[block, 2 * local + 1, :, GROUP : 2 * GROUP] = cosine
    table = table.reshape(blocks * ROWS, groups * 128).astype(np.float32)
    high = table.astype(jnp.bfloat16)
    low = (table - high.astype(np.float32)).astype(jnp.bfloat16)
    return np.stack([high, low])


def fine_kernel(x_ref, table_ref, out_ref, fine_ref):
    for h in range(2):
        rows = x_ref[:, h].astype(F32).reshape(8 * ROWS, 128)
        turned = rows.T.astype(BF16)
        fine = lax.dot_general(turned, table_ref[0], NN, preferred_element_type=F32)
        fine = fine + lax.dot_general(turned, table_ref[1], NN, preferred_element_type=F32)
        for g in range(4):
            fine_ref[h, g] = fine[:, g * 128 : g * 128 + 128]
        for j in range(4):
            for g in range(4):
                for pol in range(2):
                    piece = fine_ref[h, g, pl.ds(j * SIGS + pol, 16, stride=2), :]
                    out_ref[(h * 4 + j) * 4 + g, :, pol * 128 : pol * 128 + 128] = piece.astype(BF16)


def pairs_kernel(map_ref, pairs_ref, x_ref, out_ref, ordered_ref, own_ref, turned_ref, made, sems):
    tiles = made.shape[0]
    stations = x_ref.shape[0]
    place = lax.broadcasted_iota(jnp.int32, (BLOCK, stations), 0)
    lane = lax.broadcasted_iota(jnp.int32, (BLOCK, 128), 1)
    for part in range(stations // BLOCK):
        chosen = jnp.where(map_ref[...] == place + part * BLOCK, 1.0, 0.0).astype(BF16)
        rows = lax.dot_general(chosen, x_ref[...], NN, preferred_element_type=F32)
        for pol in range(2):
            ordered_ref[pl.ds(part * 2 * BLOCK + pol, BLOCK, stride=2), :] = rows[
                :, pol * 128 : pol * 128 + 128
            ]
        for block in range(2):
            span = slice((part * 2 + block) * BLOCK, (part * 2 + block + 1) * BLOCK)
            value = ordered_ref[span, :]
            own_ref[span, :] = value.astype(BF16)
            turned = jnp.where(
                lane < GROUP, -pltpu.roll(value, 128 - GROUP, 1), pltpu.roll(value, GROUP, 1)
            )
            turned_ref[span, :] = turned.astype(BF16)

    def send(tile):
        return pltpu.make_async_copy(made.at[tile], out_ref.at[0, tile], sems.at[tile])

    @pl.loop(0, tiles, unroll=12)
    def _(tile):
        left = pl.ds(pl.multiple_of(pairs_ref[0, tile] * 128, 128), 128)
        right = pl.ds(pl.multiple_of(pairs_ref[1, tile] * 128, 128), 128)
        other = jnp.concatenate([own_ref[right, :], turned_ref[right, :]], axis=0)
        product = lax.dot_general(own_ref[left, :], other, NT, preferred_element_type=F32)
        product = product * (1.0 / GROUP)
        made[tile, 0] = product[:, :128]
        made[tile, 1] = product[:, 128:]
        send(tile).start()

    @pl.loop(0, tiles)
    def _(tile):
        send(tile).wait()


def columns(rows):
    return [pltpu.VMEM((rows, 256), BF16)] * 6


def front_call(x, proto, kept, beam):
    return pl.pallas_call(
        front_kernel,
        out_shape=jax.ShapeDtypeStruct((8, 2, ROWS, 128), BF16),
        in_specs=[anywhere()] * 4,
        out_specs=vmem(),
        scratch_shapes=[
            pltpu.VMEM((LOCAL * COLS, SIGS, 128), BF16),
            pltpu.VMEM(proto.shape, F32),
            pltpu.VMEM(beam.shape, F32),
            pltpu.VMEM((1, KEPT), jnp.int32),
            pltpu.VMEM((256, FRAME), BF16),
            pltpu.VMEM((4 * KEPT, 128), F32),
            pltpu.VMEM((2 * KEPT, 128), F32),
            pltpu.VMEM((128, PADDED), F32),
            pltpu.VMEM((16 * ROWS, 128), F32),
            *[pltpu.VMEM((PADDED, 256), BF16)] * 6,
            pltpu.SemaphoreType.DMA((16,)),
            pltpu.SemaphoreType.DMA((3,)),
        ],
        compiler_params=granted(16),
        name="front",
    )(x, proto, kept, beam)


def fine_call(turned, table):
    return pl.pallas_call(
        fine_kernel,
        out_shape=jax.ShapeDtypeStruct((32, 16, 256), BF16),
        in_specs=[vmem()] * 2,
        out_specs=vmem(),
        scratch_shapes=[pltpu.VMEM((2, 4, 128, 128), F32)],
        compiler_params=granted(8),
        name="fine",
    )(turned, table)


def pairs_call(station_map, tile_pairs, rows):
    tiles = tile_pairs.shape[1]
    return pl.pallas_call(
        pairs_kernel,
        out_shape=jax.ShapeDtypeStruct((1, tiles, 2, BLOCK, BLOCK), F32),
        in_specs=[vmem(), smem(), vmem()],
        out_specs=anywhere(),
        scratch_shapes=[
            pltpu.VMEM((1024, 128), F32),
            pltpu.VMEM((1024, 128), BF16),
            pltpu.VMEM((1024, 128), BF16),
            pltpu.VMEM((tiles, 2, BLOCK, BLOCK), F32),
            pltpu.SemaphoreType.DMA((tiles,)),
        ],
        compiler_params=granted(10),
        name="pairs",
    )(station_map, tile_pairs, rows)


def kept_in_hbm(value):
    return pltpu.with_memory_space_constraint(value, pltpu.HBM)


def shards(voltages, prototype, kept_channels, beam_jones, station_map, tile_pairs):
    stations = voltages.shape[0]
    x = voltages.reshape(stations, 2, LOCAL * COLS, 128).transpose(0, 2, 1, 3)
    beamed = front_call(
        kept_in_hbm(x),
        kept_in_hbm(prototype),
        kept_in_hbm(kept_channels.reshape(1, KEPT)),
        kept_in_hbm(beam_jones.reshape(128, KEPT)),
    )
    turned = lax.all_to_all(beamed, "tm", 0, 0, tiled=True)
    fine = fine_call(turned, jnp.asarray(fine_table()))
    rows = lax.all_to_all(fine, "stn", 0, 0, tiled=True)
    return pairs_call(station_map.reshape(1, -1), tile_pairs.T, rows.reshape(-1, 256))


def solution(mesh):
    placed = (P("stn", None, "tm"), P(), P(), P("stn", None, None, None, None), P(), P())
    return jax.shard_map(
        shards,
        mesh=mesh,
        in_specs=placed,
        out_specs=P(("tm", "stn"), None, None, None, None),
        check_vma=False,
    )
```

```python
import functools
import math

import jax
import jax.numpy as jnp
import numpy as np
from jax import lax
from jax.experimental import pallas as pl
from jax.experimental.pallas import tpu as pltpu
from jax.sharding import PartitionSpec as P

GROUP = 54
BLOCK = 128
TAPS = 12
FRAME = 768
COLS = FRAME // 128
LOCAL = 27
SPREAD = LOCAL + TAPS - 1
TILES = 10
STEPS = 10
FIRST_TM = 5
FIRST_STN = 22
PADDED = 1536
SIGS = 32
KEPT = 64
ROWS = 80

F32 = jnp.float32
BF16 = jnp.bfloat16
NT = (((1,), (1,)), ((), ()))
NN = (((1,), (0,)), ((), ()))


def vmem():
    return pl.BlockSpec(memory_space=pltpu.VMEM)


def anywhere():
    return pl.BlockSpec(memory_space=pltpu.HBM)


def smem():
    return pl.BlockSpec(memory_space=pltpu.SMEM)


def granted(mebibytes):
    return pltpu.CompilerParams(vmem_limit_bytes=mebibytes * 2**20)


def split(value):
    high = value.astype(BF16)
    return high, (value - high.astype(F32)).astype(BF16)


def turn(phase):
    quarter = jnp.floor((phase + 96.0) * (1.0 / 192.0))
    angle = (phase - quarter * 192.0) * (2.0 * math.pi / FRAME)
    square = angle * angle
    sine = 1.0 / 362880.0
    for term in (-1.0 / 5040.0, 1.0 / 120.0, -1.0 / 6.0, 1.0):
        sine = sine * square + term
    sine = sine * angle
    cosine = 1.0 / 40320.0
    for term in (-1.0 / 720.0, 1.0 / 24.0, -0.5, 1.0):
        cosine = cosine * square + term
    quarter = quarter.astype(jnp.int32) & 3
    odd = (quarter & 1) == 1
    first = jnp.where(odd, sine, cosine)
    second = jnp.where(odd, cosine, sine)
    flip = (quarter == 1) | (quarter == 2)
    return jnp.where(flip, -first, first), jnp.where(quarter >= 2, second, -second)


def coarse_table(kept_ref, turned_ref, w_ref):
    turned_ref[:KEPT, :] = jnp.broadcast_to(kept_ref[...].astype(F32), (128, KEPT)).T
    lane = lax.broadcasted_iota(jnp.int32, (8, 128), 1).astype(F32)
    factor = 1.0 / math.sqrt(FRAME)
    for j in range(4):
        for h in range(2):
            kept = turned_ref[pl.ds(4 * h + j, 8, stride=8), :]
            re, im = turn(kept * lane)
            re, im = re * factor, im * factor
            step_re, step_im = turn(kept * 128.0)
            row = (j * 2 + h) * 8
            for col in range(COLS):
                span = slice(col * 128, col * 128 + 128)
                for part, value in enumerate((re, im)):
                    high, low = split(value)
                    w_ref[part * KEPT + row : part * KEPT + row + 8, span] = high
                    w_ref[128 + part * KEPT + row : 128 + part * KEPT + row + 8, span] = low
                re, im = re * step_re - im * step_im, re * step_im + im * step_re


def filter_column(x_ref, proto_ref, high_ref, low_ref, col, half, lane_at, outputs):
    taken = pl.ds(pl.multiple_of(col * 128, 128), 128)
    put = pl.ds(pl.multiple_of(lane_at * 128, 128), 128)
    side = pl.ds(pl.multiple_of(half * 16, 16), 16)
    taps = [jnp.broadcast_to(proto_ref[k : k + 1, taken], (16, 128)) for k in range(TAPS)]
    sums, left = {}, {}
    for out in outputs.values():
        left[out] = left.get(out, 0) + 1
    for n in range(LOCAL):
        x = x_ref[n * COLS + col, side, :].astype(F32)
        for k in range(TAPS):
            if (k, n) not in outputs:
                continue
            out = outputs[k, n]
            sums[out] = sums[out] + taps[k] * x if out in sums else taps[k] * x
            left[out] -= 1
            if left[out] == 0:
                high, low = split(sums.pop(out))
                rows = pl.ds(pl.multiple_of(out * SIGS + half * 16, 16), 16)
                high_ref[rows, put] = high
                low_ref[rows, put] = low


def coarse_sums(x_ref, proto_ref, w_ref, highs, lows, sums_ref, outputs):
    def transform(pair, q, chunk):
        rows = pl.ds(pl.multiple_of(q * chunk, chunk), chunk)
        span = slice(pair * 256, pair * 256 + 256)
        both = lax.dot_general(
            w_ref[:, span], highs[pair][rows, :], NT, preferred_element_type=F32
        )
        rest = lax.dot_general(
            w_ref[:128, span], lows[pair][rows, :], NT, preferred_element_type=F32
        )
        value = both[:128] + both[128:] + rest
        if pair > 0:
            value = value + sums_ref[:, rows]
        sums_ref[:, rows] = value

    for pair in range(COLS // 2):

        @pl.loop(0, 4)
        def _(q):
            if pair > 0:
                transform(pair - 1, q, PADDED // 4)
            filter_column(
                x_ref, proto_ref, highs[pair], lows[pair],
                pair * 2 + q // 2, q % 2, q // 2, outputs,
            )

    for q in range(STEPS):
        transform(COLS // 2 - 1, q, TILES * 128 // STEPS)


def beam_and_deal(load, jones_ref, dealt_ref, tiles, stride):
    lane = lax.broadcasted_iota(jnp.int32, (8, 128), 1)
    even = lane % 2 == 0
    low_half = lane < 64
    even_chunk = (lane // 32) % 2 == 0

    def swap(value):
        return jnp.where(even, pltpu.roll(value, 127, 1), pltpu.roll(value, 1, 1))

    def beam(tile, row):
        re, im = load(row, tile), load(KEPT + row, tile)
        swap_re, swap_im = swap(re), swap(im)
        own_re, own_im, cross_re, cross_im = (
            jones_ref[n * KEPT + row : n * KEPT + row + 8, :] for n in range(4)
        )
        return (
            own_re * re - own_im * im + cross_re * swap_re - cross_im * swap_im,
            own_re * im + own_im * re + cross_re * swap_im + cross_im * swap_re,
        )

    for tile in range(tiles):
        for h in range(2):
            beams = [beam(tile, (j * 2 + h) * 8) for j in range(4)]
            for part in range(2):
                v = [beams[j][part] for j in range(4)]
                u = [None] * 4
                for j in range(2):
                    u[j] = jnp.where(low_half, v[j], pltpu.roll(v[j + 2], 64, 1))
                    u[j + 2] = jnp.where(low_half, pltpu.roll(v[j], 64, 1), v[j + 2])
                for i in (0, 2):
                    first = jnp.where(even_chunk, u[i], pltpu.roll(u[i + 1], 32, 1))
                    second = jnp.where(even_chunk, pltpu.roll(u[i], 96, 1), u[i + 1])
                    for n, value in enumerate((first, second)):
                        row = h * (stride // 2) + (tile * 4 + i + n) * 2 + part
                        dealt_ref[pl.ds(row, 8, stride=stride), :] = value


MAIN_OUT = {
    (k, n): n + TAPS - 1 - k
    for n in range(LOCAL)
    for k in range(TAPS)
    if n + TAPS - 1 - k < LOCAL
}


def clear(refs, first, last):
    for ref in refs:
        ref[first:last, :] = jnp.zeros((last - first, 256), BF16)


def deal_beam(beam_ref, turned_ref, jones_ref):
    side = lax.broadcasted_iota(jnp.int32, (8, 128), 1) % 2 == 0
    for part in range(2):
        for q in range(2):
            rows = beam_ref[pl.ds(q * 2 + part, SIGS, stride=4), :]
            wide = jnp.concatenate([rows.T] * 4, axis=1)
            turned_ref[q * KEPT : q * KEPT + KEPT, :] = wide
        for j in range(4):
            for h in range(2):
                first = turned_ref[pl.ds(4 * h + j, 8, stride=8), :]
                second = turned_ref[pl.ds(KEPT + 4 * h + j, 8, stride=8), :]
                row = (j * 2 + h) * 8
                own = jnp.where(side, first, second)
                cross = jnp.where(side, second, first)
                jones_ref[part * KEPT + row : part * KEPT + row + 8, :] = own
                jones_ref[(2 + part) * KEPT + row : (2 + part) * KEPT + row + 8, :] = cross


def front_kernel(
    x_ref, proto_in, kept_in, beam_in, out_ref, xt_ref, proto_ref, beam_ref, kept_ref,
    w_ref, jones_ref, turned_ref, sums_ref, dealt_ref, h0, h1, h2, l0, l1, l2, sems, more,
):
    stations = x_ref.shape[0]
    rows = [
        pltpu.make_async_copy(x_ref.at[s], xt_ref.at[:, pl.ds(2 * s, 2)], sems.at[s])
        for s in range(stations)
    ]
    kept_copy = pltpu.make_async_copy(kept_in, kept_ref, more.at[0])
    proto_copy = pltpu.make_async_copy(proto_in, proto_ref, more.at[1])
    beam_copy = pltpu.make_async_copy(beam_in, beam_ref, more.at[2])
    for copy in [kept_copy, beam_copy, proto_copy] + rows:
        copy.start()
    clear((h0, h1, h2, l0, l1, l2), SPREAD * SIGS, TILES * 128)
    kept_copy.wait()
    beam_copy.wait()
    coarse_table(kept_ref, turned_ref, w_ref)
    deal_beam(beam_ref, turned_ref, jones_ref)
    for copy in [proto_copy] + rows:
        copy.wait()
    outputs = {(k, n): n + TAPS - 1 - k for n in range(LOCAL) for k in range(TAPS)}
    coarse_sums(
        xt_ref, proto_ref, w_ref, (h0, h1, h2), (l0, l1, l2), sums_ref, outputs,
    )
    beam_and_deal(
        lambda row, tile: sums_ref[row : row + 8, tile * 128 : tile * 128 + 128],
        jones_ref, dealt_ref, TILES, 2 * ROWS,
    )
    for d in range(8):
        for h in range(2):
            first = (d * 2 + h) * ROWS
            out_ref[(d - FIRST_TM) % 8, h] = dealt_ref[first : first + ROWS, :].astype(BF16)


def fine_table():
    blocks = 8
    length = blocks * LOCAL
    groups = length // GROUP
    table = np.zeros((blocks, ROWS, groups, 128))
    k = np.arange(length)
    for block in range(blocks):
        for local in range(SPREAD):
            frame = block * LOCAL + local
            if frame >= length:
                continue
            angle = 2.0 * np.pi * ((frame * k) % length) / length
            cosine = (np.cos(angle) / np.sqrt(length)).reshape(groups, GROUP)
            sine = (np.sin(angle) / np.sqrt(length)).reshape(groups, GROUP)
            table[block, 2 * local, :, :GROUP] = cosine
            table[block, 2 * local, :, GROUP : 2 * GROUP] = -sine
            table[block, 2 * local + 1, :, :GROUP] = sine
            table[block, 2 * local + 1, :, GROUP : 2 * GROUP] = cosine
    table = np.roll(table, -FIRST_TM, axis=0)
    table = table.reshape(blocks * ROWS, groups * 128).astype(np.float32)
    high = table.astype(jnp.bfloat16)
    low = (table - high.astype(np.float32)).astype(jnp.bfloat16)
    return np.stack([high, low])


def fine_kernel(x_ref, table_ref, out_ref, fine_ref):
    for h in range(2):
        rows = x_ref[:, h].astype(F32).reshape(8 * ROWS, 128)
        turned = rows.T.astype(BF16)
        fine = lax.dot_general(turned, table_ref[0], NN, preferred_element_type=F32)
        fine = fine + lax.dot_general(turned, table_ref[1], NN, preferred_element_type=F32)
        for g in range(4):
            fine_ref[h, g] = fine[:, g * 128 : g * 128 + 128]
        for j in range(4):
            for g in range(4):
                for pol in range(2):
                    piece = fine_ref[h, g, pl.ds(j * SIGS + pol, 16, stride=2), :]
                    at = ((h * 4 + j) * 4 + g - FIRST_STN) % 32
                    out_ref[at, :, pol * 128 : pol * 128 + 128] = piece.astype(BF16)


def pairs_kernel(map_ref, pairs_ref, x_ref, out_ref, ordered_ref, own_ref, turned_ref, made, sems):
    tiles = made.shape[0]
    stations = x_ref.shape[0]
    placed = pltpu.roll(map_ref[...], stations - FIRST_STN * (stations // 32), 1)
    place = lax.broadcasted_iota(jnp.int32, (BLOCK, stations), 0)
    lane = lax.broadcasted_iota(jnp.int32, (BLOCK, 128), 1)
    for part in range(stations // BLOCK):
        chosen = jnp.where(placed == place + part * BLOCK, 1.0, 0.0).astype(BF16)
        rows = lax.dot_general(chosen, x_ref[...], NN, preferred_element_type=F32)
        for pol in range(2):
            ordered_ref[pl.ds(part * 2 * BLOCK + pol, BLOCK, stride=2), :] = rows[
                :, pol * 128 : pol * 128 + 128
            ]
        for block in range(2):
            span = slice((part * 2 + block) * BLOCK, (part * 2 + block + 1) * BLOCK)
            value = ordered_ref[span, :]
            own_ref[span, :] = value.astype(BF16)
            turned = jnp.where(
                lane < GROUP, -pltpu.roll(value, 128 - GROUP, 1), pltpu.roll(value, GROUP, 1)
            )
            turned_ref[span, :] = turned.astype(BF16)

    def send(tile):
        return pltpu.make_async_copy(made.at[tile], out_ref.at[0, tile], sems.at[tile])

    @pl.loop(0, tiles, unroll=12)
    def _(tile):
        left = pl.ds(pl.multiple_of(pairs_ref[0, tile] * 128, 128), 128)
        right = pl.ds(pl.multiple_of(pairs_ref[1, tile] * 128, 128), 128)
        other = jnp.concatenate([own_ref[right, :], turned_ref[right, :]], axis=0)
        product = lax.dot_general(own_ref[left, :], other, NT, preferred_element_type=F32)
        product = product * (1.0 / GROUP)
        made[tile, 0] = product[:, :128]
        made[tile, 1] = product[:, 128:]
        send(tile).start()

    @pl.loop(0, tiles)
    def _(tile):
        send(tile).wait()


def columns(rows):
    return [pltpu.VMEM((rows, 256), BF16)] * 6


def front_call(x, proto, kept, beam):
    return pl.pallas_call(
        front_kernel,
        out_shape=jax.ShapeDtypeStruct((8, 2, ROWS, 128), BF16),
        in_specs=[anywhere()] * 4,
        out_specs=vmem(),
        scratch_shapes=[
            pltpu.VMEM((LOCAL * COLS, SIGS, 128), BF16),
            pltpu.VMEM(proto.shape, F32),
            pltpu.VMEM(beam.shape, F32),
            pltpu.VMEM((1, KEPT), jnp.int32),
            pltpu.VMEM((256, FRAME), BF16),
            pltpu.VMEM((4 * KEPT, 128), F32),
            pltpu.VMEM((2 * KEPT, 128), F32),
            pltpu.VMEM((128, PADDED), F32),
            pltpu.VMEM((16 * ROWS, 128), F32),
            *[pltpu.VMEM((PADDED, 256), BF16)] * 6,
            pltpu.SemaphoreType.DMA((16,)),
            pltpu.SemaphoreType.DMA((3,)),
        ],
        compiler_params=granted(16),
        name="front",
    )(x, proto, kept, beam)


def fine_call(turned, table):
    return pl.pallas_call(
        fine_kernel,
        out_shape=jax.ShapeDtypeStruct((32, 16, 256), BF16),
        in_specs=[vmem()] * 2,
        out_specs=vmem(),
        scratch_shapes=[pltpu.VMEM((2, 4, 128, 128), F32)],
        compiler_params=granted(8),
        name="fine",
    )(turned, table)


def pairs_call(station_map, tile_pairs, rows):
    tiles = tile_pairs.shape[1]
    return pl.pallas_call(
        pairs_kernel,
        out_shape=jax.ShapeDtypeStruct((1, tiles, 2, BLOCK, BLOCK), F32),
        in_specs=[vmem(), smem(), vmem()],
        out_specs=anywhere(),
        scratch_shapes=[
            pltpu.VMEM((1024, 128), F32),
            pltpu.VMEM((1024, 128), BF16),
            pltpu.VMEM((1024, 128), BF16),
            pltpu.VMEM((tiles, 2, BLOCK, BLOCK), F32),
            pltpu.SemaphoreType.DMA((tiles,)),
        ],
        compiler_params=granted(10),
        name="pairs",
    )(station_map, tile_pairs, rows)


def kept_in_hbm(value):
    return pltpu.with_memory_space_constraint(value, pltpu.HBM)


def exchange(value, axis, first):
    count = lax.axis_size(axis)
    group = [(first + n) % count for n in range(count)]
    return lax.all_to_all(value, axis, 0, 0, tiled=True, axis_index_groups=[group])


def shards(voltages, prototype, kept_channels, beam_jones, station_map, tile_pairs):
    stations = voltages.shape[0]
    x = voltages.reshape(stations, 2, LOCAL * COLS, 128).transpose(0, 2, 1, 3)
    beamed = front_call(
        kept_in_hbm(x),
        kept_in_hbm(prototype),
        kept_in_hbm(kept_channels.reshape(1, KEPT)),
        kept_in_hbm(beam_jones.reshape(128, KEPT)),
    )
    turned = exchange(beamed, "tm", FIRST_TM)
    fine = fine_call(turned, jnp.asarray(fine_table()))
    rows = exchange(fine, "stn", FIRST_STN)
    return pairs_call(station_map.reshape(1, -1), tile_pairs.T, rows.reshape(-1, 256))


def solution(mesh):
    placed = (P("stn", None, "tm"), P(), P(), P("stn", None, None, None, None), P(), P())
    return jax.shard_map(
        shards,
        mesh=mesh,
        in_specs=placed,
        out_specs=P(("tm", "stn"), None, None, None, None),
        check_vma=False,
    )
```

```python
import functools
import math

import jax
import jax.numpy as jnp
import numpy as np
from jax import lax
from jax.experimental import pallas as pl
from jax.experimental.pallas import tpu as pltpu
from jax.sharding import PartitionSpec as P

GROUP = 54
BLOCK = 128
TAPS = 12
FRAME = 768
COLS = FRAME // 128
LOCAL = 27
SPREAD = LOCAL + TAPS - 1
TILES = 10
STEPS = 10
FIRST_TM = 5
FIRST_STN = 22
PADDED = 1536
SIGS = 32
KEPT = 64
ROWS = 80

F32 = jnp.float32
BF16 = jnp.bfloat16
NT = (((1,), (1,)), ((), ()))
NN = (((1,), (0,)), ((), ()))


def vmem():
    return pl.BlockSpec(memory_space=pltpu.VMEM)


def anywhere():
    return pl.BlockSpec(memory_space=pltpu.HBM)


def smem():
    return pl.BlockSpec(memory_space=pltpu.SMEM)


def granted(mebibytes):
    return pltpu.CompilerParams(vmem_limit_bytes=mebibytes * 2**20)


def split(value):
    high = value.astype(BF16)
    return high, (value - high.astype(F32)).astype(BF16)


def turn(phase):
    quarter = jnp.floor((phase + 96.0) * (1.0 / 192.0))
    angle = (phase - quarter * 192.0) * (2.0 * math.pi / FRAME)
    square = angle * angle
    sine = 1.0 / 362880.0
    for term in (-1.0 / 5040.0, 1.0 / 120.0, -1.0 / 6.0, 1.0):
        sine = sine * square + term
    sine = sine * angle
    cosine = 1.0 / 40320.0
    for term in (-1.0 / 720.0, 1.0 / 24.0, -0.5, 1.0):
        cosine = cosine * square + term
    quarter = quarter.astype(jnp.int32) & 3
    odd = (quarter & 1) == 1
    first = jnp.where(odd, sine, cosine)
    second = jnp.where(odd, cosine, sine)
    flip = (quarter == 1) | (quarter == 2)
    return jnp.where(flip, -first, first), jnp.where(quarter >= 2, second, -second)


def coarse_table(kept_ref, turned_ref, w_ref):
    turned_ref[:KEPT, :] = jnp.broadcast_to(kept_ref[...].astype(F32), (128, KEPT)).T
    lane = lax.broadcasted_iota(jnp.int32, (8, 128), 1).astype(F32)
    factor = 1.0 / math.sqrt(FRAME)
    for j in range(4):
        for h in range(2):
            kept = turned_ref[pl.ds(4 * h + j, 8, stride=8), :]
            re, im = turn(kept * lane)
            re, im = re * factor, im * factor
            step_re, step_im = turn(kept * 128.0)
            row = (j * 2 + h) * 8
            for col in range(COLS):
                span = slice(col * 128, col * 128 + 128)
                for part, value in enumerate((re, im)):
                    high, low = split(value)
                    w_ref[part * KEPT + row : part * KEPT + row + 8, span] = high
                    w_ref[128 + part * KEPT + row : 128 + part * KEPT + row + 8, span] = low
                re, im = re * step_re - im * step_im, re * step_im + im * step_re


def filter_column(x_ref, proto_ref, high_ref, low_ref, col, half, lane_at, outputs):
    taken = pl.ds(pl.multiple_of(col * 128, 128), 128)
    put = pl.ds(pl.multiple_of(lane_at * 128, 128), 128)
    side = pl.ds(pl.multiple_of(half * 16, 16), 16)
    taps = [jnp.broadcast_to(proto_ref[k : k + 1, taken], (16, 128)) for k in range(TAPS)]
    sums, left = {}, {}
    for out in outputs.values():
        left[out] = left.get(out, 0) + 1
    for n in range(LOCAL):
        x = x_ref[n * COLS + col, side, :].astype(F32)
        for k in range(TAPS):
            if (k, n) not in outputs:
                continue
            out = outputs[k, n]
            sums[out] = sums[out] + taps[k] * x if out in sums else taps[k] * x
            left[out] -= 1
            if left[out] == 0:
                high, low = split(sums.pop(out))
                rows = pl.ds(pl.multiple_of(out * SIGS + half * 16, 16), 16)
                high_ref[rows, put] = high
                low_ref[rows, put] = low


def coarse_sums(x_ref, proto_ref, w_ref, highs, lows, sums_ref, outputs):
    def transform(pair, q, chunk):
        rows = pl.ds(pl.multiple_of(q * chunk, chunk), chunk)
        span = slice(pair * 256, pair * 256 + 256)
        both = lax.dot_general(
            w_ref[:, span], highs[pair][rows, :], NT, preferred_element_type=F32
        )
        rest = lax.dot_general(
            w_ref[:128, span], lows[pair][rows, :], NT, preferred_element_type=F32
        )
        value = both[:128] + both[128:] + rest
        if pair > 0:
            value = value + sums_ref[:, rows]
        sums_ref[:, rows] = value

    for pair in range(COLS // 2):

        @pl.loop(0, 4)
        def _(q):
            if pair > 0:
                transform(pair - 1, q, PADDED // 4)
            filter_column(
                x_ref, proto_ref, highs[pair], lows[pair],
                pair * 2 + q // 2, q % 2, q // 2, outputs,
            )

    for q in range(STEPS):
        transform(COLS // 2 - 1, q, TILES * 128 // STEPS)


def beam_and_deal(load, jones_ref, dealt_ref, tiles, stride):
    lane = lax.broadcasted_iota(jnp.int32, (8, 128), 1)
    even = lane % 2 == 0
    low_half = lane < 64
    even_chunk = (lane // 32) % 2 == 0

    def swap(value):
        return jnp.where(even, pltpu.roll(value, 127, 1), pltpu.roll(value, 1, 1))

    def beam(tile, row):
        re, im = load(row, tile), load(KEPT + row, tile)
        swap_re, swap_im = swap(re), swap(im)
        own_re, own_im, cross_re, cross_im = (
            jones_ref[n * KEPT + row : n * KEPT + row + 8, :] for n in range(4)
        )
        return (
            own_re * re - own_im * im + cross_re * swap_re - cross_im * swap_im,
            own_re * im + own_im * re + cross_re * swap_im + cross_im * swap_re,
        )

    for tile in range(tiles):
        for h in range(2):
            beams = [beam(tile, (j * 2 + h) * 8) for j in range(4)]
            for part in range(2):
                v = [beams[j][part] for j in range(4)]
                u = [None] * 4
                for j in range(2):
                    u[j] = jnp.where(low_half, v[j], pltpu.roll(v[j + 2], 64, 1))
                    u[j + 2] = jnp.where(low_half, pltpu.roll(v[j], 64, 1), v[j + 2])
                for i in (0, 2):
                    first = jnp.where(even_chunk, u[i], pltpu.roll(u[i + 1], 32, 1))
                    second = jnp.where(even_chunk, pltpu.roll(u[i], 96, 1), u[i + 1])
                    for n, value in enumerate((first, second)):
                        row = h * (stride // 2) + (tile * 4 + i + n) * 2 + part
                        dealt_ref[pl.ds(row, 8, stride=stride), :] = value


MAIN_OUT = {
    (k, n): n + TAPS - 1 - k
    for n in range(LOCAL)
    for k in range(TAPS)
    if n + TAPS - 1 - k < LOCAL
}


def clear(refs, first, last):
    for ref in refs:
        ref[first:last, :] = jnp.zeros((last - first, 256), BF16)


def deal_beam(beam_ref, turned_ref, jones_ref):
    side = lax.broadcasted_iota(jnp.int32, (8, 128), 1) % 2 == 0
    for part in range(2):
        for q in range(2):
            rows = beam_ref[pl.ds(q * 2 + part, SIGS, stride=4), :]
            wide = jnp.concatenate([rows.T] * 4, axis=1)
            turned_ref[q * KEPT : q * KEPT + KEPT, :] = wide
        for j in range(4):
            for h in range(2):
                first = turned_ref[pl.ds(4 * h + j, 8, stride=8), :]
                second = turned_ref[pl.ds(KEPT + 4 * h + j, 8, stride=8), :]
                row = (j * 2 + h) * 8
                own = jnp.where(side, first, second)
                cross = jnp.where(side, second, first)
                jones_ref[part * KEPT + row : part * KEPT + row + 8, :] = own
                jones_ref[(2 + part) * KEPT + row : (2 + part) * KEPT + row + 8, :] = cross


def front_kernel(
    x_ref, proto_in, kept_in, beam_in, out_ref, xt_ref, proto_ref, beam_ref, kept_ref,
    w_ref, jones_ref, turned_ref, sums_ref, dealt_ref, h0, h1, h2, l0, l1, l2, sems, more,
):
    stations = x_ref.shape[0]
    rows = [
        pltpu.make_async_copy(x_ref.at[s], xt_ref.at[:, pl.ds(2 * s, 2)], sems.at[s])
        for s in range(stations)
    ]
    kept_copy = pltpu.make_async_copy(kept_in, kept_ref, more.at[0])
    proto_copy = pltpu.make_async_copy(proto_in, proto_ref, more.at[1])
    beam_copy = pltpu.make_async_copy(
        beam_in, beam_ref.at[pl.ds(0, beam_in.shape[0])], more.at[2]
    )
    for copy in [kept_copy, beam_copy, proto_copy] + rows:
        copy.start()
    clear((h0, h1, h2, l0, l1, l2), SPREAD * SIGS, TILES * 128)
    kept_copy.wait()
    beam_copy.wait()
    coarse_table(kept_ref, turned_ref, w_ref)
    deal_beam(beam_ref, turned_ref, jones_ref)
    for copy in [proto_copy] + rows:
        copy.wait()
    outputs = {(k, n): n + TAPS - 1 - k for n in range(LOCAL) for k in range(TAPS)}
    coarse_sums(
        xt_ref, proto_ref, w_ref, (h0, h1, h2), (l0, l1, l2), sums_ref, outputs,
    )
    beam_and_deal(
        lambda row, tile: sums_ref[row : row + 8, tile * 128 : tile * 128 + 128],
        jones_ref, dealt_ref, TILES, 2 * ROWS,
    )
    for d in range(8):
        for h in range(2):
            first = (d * 2 + h) * ROWS
            out_ref[(d - FIRST_TM) % 8, h] = dealt_ref[first : first + ROWS, :].astype(BF16)


def fine_table():
    blocks = 8
    length = blocks * LOCAL
    groups = length // GROUP
    table = np.zeros((blocks, ROWS, groups, 128))
    k = np.arange(length)
    for block in range(blocks):
        for local in range(SPREAD):
            frame = block * LOCAL + local
            if frame >= length:
                continue
            angle = 2.0 * np.pi * ((frame * k) % length) / length
            cosine = (np.cos(angle) / np.sqrt(length)).reshape(groups, GROUP)
            sine = (np.sin(angle) / np.sqrt(length)).reshape(groups, GROUP)
            table[block, 2 * local, :, :GROUP] = cosine
            table[block, 2 * local, :, GROUP : 2 * GROUP] = -sine
            table[block, 2 * local + 1, :, :GROUP] = sine
            table[block, 2 * local + 1, :, GROUP : 2 * GROUP] = cosine
    table = np.roll(table, -FIRST_TM, axis=0)
    table = table.reshape(blocks * ROWS, groups * 128).astype(np.float32)
    high = table.astype(jnp.bfloat16)
    low = (table - high.astype(np.float32)).astype(jnp.bfloat16)
    return np.stack([high, low])


def fine_kernel(x_ref, table_ref, out_ref, fine_ref):
    for h in range(2):
        rows = x_ref[:, h].astype(F32).reshape(8 * ROWS, 128)
        turned = rows.T.astype(BF16)
        fine = lax.dot_general(turned, table_ref[0], NN, preferred_element_type=F32)
        fine = fine + lax.dot_general(turned, table_ref[1], NN, preferred_element_type=F32)
        for g in range(4):
            fine_ref[h, g, :128, :] = fine[:, g * 128 : g * 128 + 128]
        for j in range(4):
            for g in range(4):
                for pol in range(2):
                    piece = fine_ref[h, g, pl.ds(j * SIGS + pol, 16, stride=2), :]
                    at = ((h * 4 + j) * 4 + g - FIRST_STN) % 32
                    out_ref[at, :, pol * 128 : pol * 128 + 128] = piece.astype(BF16)


def pairs_kernel(map_ref, pairs_ref, x_ref, out_ref, ordered_ref, own_ref, turned_ref, made, sems):
    tiles = made.shape[0]
    stations = x_ref.shape[0]
    placed = pltpu.roll(map_ref[...], stations - FIRST_STN * (stations // 32), 1)
    place = lax.broadcasted_iota(jnp.int32, (BLOCK, stations), 0)
    lane = lax.broadcasted_iota(jnp.int32, (BLOCK, 128), 1)
    for part in range(stations // BLOCK):
        chosen = jnp.where(placed == place + part * BLOCK, 1.0, 0.0).astype(BF16)
        rows = lax.dot_general(chosen, x_ref[...], NN, preferred_element_type=F32)
        for pol in range(2):
            ordered_ref[pl.ds(part * 2 * BLOCK + pol, BLOCK, stride=2), :] = rows[
                :, pol * 128 : pol * 128 + 128
            ]
        for block in range(2):
            span = slice((part * 2 + block) * BLOCK, (part * 2 + block + 1) * BLOCK)
            value = ordered_ref[span, :]
            own_ref[span, :] = value.astype(BF16)
            turned = jnp.where(
                lane < GROUP, -pltpu.roll(value, 128 - GROUP, 1), pltpu.roll(value, GROUP, 1)
            )
            turned_ref[span, :] = turned.astype(BF16)

    def send(tile):
        return pltpu.make_async_copy(made.at[tile], out_ref.at[0, tile], sems.at[tile])

    @pl.loop(0, tiles, unroll=12)
    def _(tile):
        left = pl.ds(pl.multiple_of(pairs_ref[0, tile] * 128, 128), 128)
        right = pl.ds(pl.multiple_of(pairs_ref[1, tile] * 128, 128), 128)
        other = jnp.concatenate([own_ref[right, :], turned_ref[right, :]], axis=0)
        product = lax.dot_general(own_ref[left, :], other, NT, preferred_element_type=F32)
        product = product * (1.0 / GROUP)
        made[tile, 0] = product[:, :128]
        made[tile, 1] = product[:, 128:]
        send(tile).start()

    @pl.loop(0, tiles)
    def _(tile):
        send(tile).wait()


def columns(rows):
    return [pltpu.VMEM((rows, 256), BF16)] * 6


def front_call(x, proto, kept, beam):
    return pl.pallas_call(
        front_kernel,
        out_shape=jax.ShapeDtypeStruct((8, 2, ROWS, 128), BF16),
        in_specs=[anywhere()] * 4,
        out_specs=vmem(),
        scratch_shapes=[
            pltpu.VMEM((LOCAL * COLS, SIGS, 128), BF16),
            pltpu.VMEM(proto.shape, F32),
            pltpu.VMEM((beam.shape[0] + 8, beam.shape[1]), F32),
            pltpu.VMEM((1, KEPT), jnp.int32),
            pltpu.VMEM((256, FRAME), BF16),
            pltpu.VMEM((4 * KEPT, 128), F32),
            pltpu.VMEM((2 * KEPT + 16, 128), F32),
            pltpu.VMEM((128, PADDED), F32),
            pltpu.VMEM((18 * ROWS, 128), F32),
            *[pltpu.VMEM((PADDED, 256), BF16)] * 6,
            pltpu.SemaphoreType.DMA((16,)),
            pltpu.SemaphoreType.DMA((3,)),
        ],
        compiler_params=granted(16),
        name="front",
    )(x, proto, kept, beam)


def fine_call(turned, table):
    return pl.pallas_call(
        fine_kernel,
        out_shape=jax.ShapeDtypeStruct((32, 16, 256), BF16),
        in_specs=[vmem()] * 2,
        out_specs=vmem(),
        scratch_shapes=[pltpu.VMEM((2, 4, 136, 128), F32)],
        compiler_params=granted(8),
        name="fine",
    )(turned, table)


def pairs_call(station_map, tile_pairs, rows):
    tiles = tile_pairs.shape[1]
    return pl.pallas_call(
        pairs_kernel,
        out_shape=jax.ShapeDtypeStruct((1, tiles, 2, BLOCK, BLOCK), F32),
        in_specs=[vmem(), smem(), vmem()],
        out_specs=anywhere(),
        scratch_shapes=[
            pltpu.VMEM((1032, 128), F32),
            pltpu.VMEM((1024, 128), BF16),
            pltpu.VMEM((1024, 128), BF16),
            pltpu.VMEM((tiles, 2, BLOCK, BLOCK), F32),
            pltpu.SemaphoreType.DMA((tiles,)),
        ],
        compiler_params=granted(10),
        name="pairs",
    )(station_map, tile_pairs, rows)


def kept_in_hbm(value):
    return pltpu.with_memory_space_constraint(value, pltpu.HBM)


def exchange(value, axis, first):
    count = lax.axis_size(axis)
    group = [(first + n) % count for n in range(count)]
    return lax.all_to_all(value, axis, 0, 0, tiled=True, axis_index_groups=[group])


def shards(voltages, prototype, kept_channels, beam_jones, station_map, tile_pairs):
    stations = voltages.shape[0]
    x = voltages.reshape(stations, 2, LOCAL * COLS, 128).transpose(0, 2, 1, 3)
    beamed = front_call(
        kept_in_hbm(x),
        kept_in_hbm(prototype),
        kept_in_hbm(kept_channels.reshape(1, KEPT)),
        kept_in_hbm(beam_jones.reshape(128, KEPT)),
    )
    turned = exchange(beamed, "tm", FIRST_TM)
    fine = fine_call(turned, jnp.asarray(fine_table()))
    rows = exchange(fine, "stn", FIRST_STN)
    return pairs_call(station_map.reshape(1, -1), tile_pairs.T, rows.reshape(-1, 256))


def solution(mesh):
    placed = (P("stn", None, "tm"), P(), P(), P("stn", None, None, None, None), P(), P())
    return jax.shard_map(
        shards,
        mesh=mesh,
        in_specs=placed,
        out_specs=P(("tm", "stn"), None, None, None, None),
        check_vma=False,
    )
```
